32 devices in a mesh: groups: 2 (over y), shape: 4 (over x, core), block: 4 (over z).
Axes of the slice: x: 2, y: 2, z: 4, core: 2. Of those that a mesh axis runs over, the one named last changes fastest.
Arguments:
- query: bfloat16 [8, 16, 2048], P(('groups', 'shape'), 'block'), parts along dimension 0, may hold values from -6 to 6
- raw_flow_keys: bfloat16 [8, 16, 2048], P(('groups', 'shape'), 'block'), parts along dimension 0, may hold values from -6 to 6
- flow_value_input: bfloat16 [8, 16, 2048], P(('groups', 'shape'), 'block'), parts along dimension 0, may hold values from -6 to 6
- query_norm_gain: float32 [128], replicated, may hold values from 1 to 2.5
- key_norm_gain: float32 [128], replicated, may hold values from 1 to 2.5
- dec_keys: bfloat16 [8, 16, 1024], P(('groups', 'shape'), 'block'), parts along dimension 0, may hold values from -6 to 6
- dec_values: bfloat16 [8, 16, 1024], P(('groups', 'shape'), 'block'), parts along dimension 0, may hold values from -6 to 6
- block_ids: int32 [8, 16], P(('groups', 'shape'), 'block'), parts along dimension 0, may hold values from 0 to 262143
- counts: int32 [8, 4], P(('groups', 'shape'), 'block'), parts along dimension 0, may hold values from 0 to 4, as said below
- page_of: int32 [8, 16], P(('groups', 'shape'), 'block'), parts along dimension 0, may hold values from 0 to 3, as said below
- point_weight: float32 [51, 1024], replicated, may hold values from -0.875 to 0.875
- point_gain: float32 [1024], replicated, may hold values from 1 to 2.5
- occupancy_weight: float32 [1024], replicated, may hold values from -0.1875 to 0.1875
Outputs:
- flow_out: bfloat16 [8, 16, 2048], P(('groups', 'shape'), 'block'), parts along dimension 0
- occupancy: float32 [8, 4, 512], P(('groups', 'shape'), 'block'), parts along dimension 0
The draws below stay inside these ranges and needn't reach their ends.
There are 2 independent parts, one for each index of `groups`. The reference program is written for one: setup_inputs(seed, part) draws one part's arguments, and reference() takes and returns one part's arrays. A program takes and returns all parts, laid end to end along the dimension named above; an argument that names none is the same for every part. Nothing has to cross between parts.
Inputs may be any that keep to these rules, and one draw needn't show every extreme that they name: Some device of every shape has 4 live slots; the counts of one shape sum to 4. `page_of`: within a shape, every page 0 to 3 is named by exactly one live slot, and the live slots of one device name pages of distinct devices; page p lies on device p // 1 of the block axis. Dead slots name any page.
All inputs are finite; a program needn't handle non-finite values.
Results may differ from the reference program's by a relative error of at most 0.0094.
Values may be sent and summed in bfloat16 or wider, within the bound.
A program may use at most 64 MiB of HBM per device.

```python
import math
import jax
import jax.numpy as jnp
from jax import lax

FLOW_HEAD_COUNT = 16
FLOW_HEAD_SIZE = 128
DEC_HEADS = 16
DEC_HEAD = 64
NFREQ = 8
RES = 512
SIDE = 8
CAP = 4
PAGES = 1
LATENT_TOKENS = 16
SHAPE_TOTAL = 4
FOURIER = 51
QB = 512
PER_SIDE = 64
GRID_BLOCKS = 262144
SLOTS = 16
PAGE_ROWS = 4


def listing(key):
    peer_count = PAGE_ROWS // PAGES
    pair_count = (peer_count - 4) // 2

    def one_shape(shape_key):
        key_a, key_b, key_c, key_d = jax.random.split(shape_key, 4)
        order_perm = jax.random.permutation(key_a, peer_count)
        shift_pair = jax.random.randint(key_b, (pair_count,), -PAGES, PAGES + 1).astype(jnp.int32)
        base_counts = jnp.concatenate([jnp.array([CAP, 0, 0, 0], jnp.int32), PAGES + shift_pair, PAGES - shift_pair]).astype(jnp.int32)
        count_row = jnp.zeros((peer_count,), jnp.int32).at[order_perm].set(base_counts)
        live_mask = (jnp.arange(CAP, dtype=jnp.int32)[None, :] < count_row[:, None]).reshape(-1)
        slot_rank = jnp.cumsum(live_mask.astype(jnp.int32)) - 1
        target = jax.random.permutation(key_c, peer_count).astype(jnp.int32)
        page_num = target[slot_rank % peer_count] * PAGES + slot_rank // peer_count
        filler = jax.random.randint(key_d, (SLOTS,), 0, PAGE_ROWS).astype(jnp.int32)
        return (count_row, jnp.where(live_mask, page_num, filler).astype(jnp.int32))
    shape_keys = jax.random.split(jax.random.fold_in(key, 4099), SHAPE_TOTAL)
    return jax.vmap(one_shape)(shape_keys)


def draw_counts(key, part):
    return listing(key)[0]


def draw_page_of(key, part):
    return listing(key)[1]


def touch_ends(values, key, least, high):
    place = [jax.random.randint(jax.random.fold_in(key, axis), (), 0, length) for axis, length in enumerate(values.shape)]
    longest = values.shape.index(max(values.shape))
    neighbour = place[:longest] + [(place[longest] + 1) % values.shape[longest]] + place[longest + 1:]
    return values.at[tuple(place)].set(least).at[tuple(neighbour)].set(high)


def shard_levels(key, extent, shards, least, high):
    def one(axis_at, shards_of):
        steps = jax.random.uniform(jax.random.fold_in(jax.random.fold_in(key, 6), axis_at), (shards_of,), jnp.float32, least / len(shards), high / len(shards))
        return jnp.repeat(jnp.exp(steps), extent[axis_at] // shards_of).reshape((-1,) + (1,) * (len(extent) - axis_at - 1))

    loudness = one(*shards[0])
    for cut in shards[1:]:
        loudness = loudness * one(*cut)
    return loudness


def gaussian(stream_key, dims, scale, bound, pieces=(), kind=jnp.bfloat16):
    values = scale * jax.random.normal(stream_key, dims, jnp.float32)
    if pieces:
        values = values * shard_levels(stream_key, dims, pieces, -0.22, 0.18)
    return jnp.clip(values, -bound, bound).astype(kind)


def setup_inputs(seed: int = 0, part: int = 0) -> dict:
    arg_keys = jax.random.split(jax.random.key(seed), 14)
    part_splits = jax.random.split(jax.random.fold_in(arg_keys[13], part), 14)
    return {
        "query": gaussian(part_splits[0], (SHAPE_TOTAL, LATENT_TOKENS, FLOW_HEAD_COUNT * FLOW_HEAD_SIZE), 1.0, 6.0, ((0, 4), (1, 4))),
        "raw_flow_keys": gaussian(part_splits[1], (SHAPE_TOTAL, LATENT_TOKENS, FLOW_HEAD_COUNT * FLOW_HEAD_SIZE), 1.0, 6.0, ((0, 4), (1, 4))),
        "flow_value_input": gaussian(part_splits[2], (SHAPE_TOTAL, LATENT_TOKENS, FLOW_HEAD_COUNT * FLOW_HEAD_SIZE), 1.0, 6.0, ((0, 4), (1, 4))),
        "query_norm_gain": jnp.clip(jnp.exp(jax.random.uniform(arg_keys[3], (FLOW_HEAD_SIZE,), jnp.float32, math.log(1.0), math.log(2.5))), 1.0, 2.5),
        "key_norm_gain": jnp.clip(jnp.exp(jax.random.uniform(arg_keys[4], (FLOW_HEAD_SIZE,), jnp.float32, math.log(1.0), math.log(2.5))), 1.0, 2.5),
        "dec_keys": gaussian(part_splits[5], (SHAPE_TOTAL, LATENT_TOKENS, DEC_HEADS * DEC_HEAD), 1.0, 6.0, ((0, 4), (1, 4))),
        "dec_values": gaussian(part_splits[6], (SHAPE_TOTAL, LATENT_TOKENS, DEC_HEADS * DEC_HEAD), 1.0, 6.0, ((0, 4), (1, 4))),
        "block_ids": touch_ends(jax.random.randint(part_splits[7], (SHAPE_TOTAL, SLOTS), 0, GRID_BLOCKS), jax.random.fold_in(part_splits[7], 1), 0, GRID_BLOCKS - 1).astype(jnp.int32),
        "counts": draw_counts(jax.random.fold_in(jax.random.fold_in(arg_keys[13], part), 71), part),
        "page_of": draw_page_of(jax.random.fold_in(jax.random.fold_in(arg_keys[13], part), 71), part),
        "point_weight": gaussian(arg_keys[10], (FOURIER, DEC_HEADS * DEC_HEAD), FOURIER ** -0.5, 0.875, (), jnp.float32),
        "point_gain": jnp.clip(jnp.exp(jax.random.uniform(arg_keys[11], (DEC_HEADS * DEC_HEAD,), jnp.float32, math.log(1.0), math.log(2.5))), 1.0, 2.5),
        "occupancy_weight": gaussian(arg_keys[12], (DEC_HEADS * DEC_HEAD,), (DEC_HEADS * DEC_HEAD) ** -0.5, 0.1875, (), jnp.float32),
    }


def norm_per_head(values_in, gain, head_count):
    flat_rows = values_in.shape[0]
    entries = values_in.astype(jnp.float32).reshape(flat_rows, head_count, -1)
    scaled = entries * lax.rsqrt(lax.optimization_barrier(jnp.mean(entries * entries, axis=-1, keepdims=True)) + 1e-06)
    return (scaled * gain).reshape(flat_rows, -1).astype(jnp.bfloat16)

def flow_attention(query, raw_flow_keys, flow_value_input, query_norm_gain, key_norm_gain):
    token_rows = query.shape[0]
    normed_queries = norm_per_head(query, query_norm_gain, FLOW_HEAD_COUNT).reshape(token_rows, FLOW_HEAD_COUNT, FLOW_HEAD_SIZE).astype(jnp.float32)
    normed_keys = norm_per_head(raw_flow_keys, key_norm_gain, FLOW_HEAD_COUNT).reshape(token_rows, FLOW_HEAD_COUNT, FLOW_HEAD_SIZE).astype(jnp.float32)
    value_all = flow_value_input.reshape(token_rows, FLOW_HEAD_COUNT, FLOW_HEAD_SIZE).astype(jnp.float32)
    score_matrix = jnp.einsum('xrb,drb->rxd', normed_queries, normed_keys) / math.sqrt(FLOW_HEAD_SIZE)
    row_maximum = lax.optimization_barrier(jnp.max(score_matrix, axis=-1, keepdims=True))
    weights = jnp.exp(score_matrix - row_maximum)
    row_sum = lax.optimization_barrier(jnp.sum(weights, axis=-1))
    rounded = lax.optimization_barrier(weights.astype(jnp.bfloat16))
    mixed = jnp.einsum('hqk,khe->hqe', rounded.astype(jnp.float32), value_all)
    result = mixed / row_sum[..., None]
    return jnp.transpose(result, (1, 0, 2)).reshape(token_rows, -1).astype(jnp.bfloat16)

def query_points(block_id):
    point_index = jnp.arange(QB, dtype=jnp.int32)
    cell_index = [block_id // (PER_SIDE * PER_SIDE) * SIDE + point_index // (SIDE * SIDE), block_id // PER_SIDE % PER_SIDE * SIDE + point_index // SIDE % SIDE, block_id % PER_SIDE * SIDE + point_index % SIDE]
    coords = jnp.stack([(cell.astype(jnp.float32) + 0.5) * (2.0 / RES) - 1.0 for cell in cell_index], 0)
    frequency = math.pi * 2.0 ** jnp.arange(NFREQ).astype(jnp.float32)
    phases = (coords[:, None, :] * frequency[None, :, None]).reshape(3 * NFREQ, QB)
    return jnp.concatenate([coords, jnp.sin(phases), jnp.cos(phases)], 0)

def decode_block(block_id, k_heads, v_heads, point_weight, point_gain, occupancy_weight):
    features = query_points(block_id)
    start_proj = lax.dot_general(features, point_weight, (((0,), (0,)), ((), ())), precision=lax.Precision.HIGHEST, preferred_element_type=jnp.float32)
    row_mean = lax.optimization_barrier(jnp.mean(start_proj, axis=-1, keepdims=True))
    centred = start_proj - row_mean
    row_var = lax.optimization_barrier(jnp.mean(centred * centred, axis=-1, keepdims=True))
    point_query = (centred * lax.rsqrt(row_var + 1e-05) * point_gain).astype(jnp.bfloat16)
    q_heads = jnp.transpose(point_query.reshape(QB, DEC_HEADS, DEC_HEAD), (1, 0, 2))

    def one_head(head_item):
        q_head, k_head, v_head = head_item
        score_matrix = jnp.dot(q_head, k_head.T, preferred_element_type=jnp.float32) / math.sqrt(DEC_HEAD)
        row_maximum = lax.optimization_barrier(jnp.max(score_matrix, axis=-1, keepdims=True))
        weights = jnp.exp(score_matrix - row_maximum)
        row_sum = lax.optimization_barrier(jnp.sum(weights, axis=-1, keepdims=True))
        mixed = jnp.dot(weights.astype(jnp.bfloat16), v_head, preferred_element_type=jnp.float32)
        return mixed / row_sum
    per_head = lax.map(one_head, (q_heads, k_heads, v_heads))
    hidden = start_proj + jnp.transpose(per_head, (1, 0, 2)).reshape(QB, -1)
    hid_mean = lax.optimization_barrier(jnp.mean(hidden, axis=-1, keepdims=True))
    hid_centred = hidden - hid_mean
    hid_var = lax.optimization_barrier(jnp.mean(hid_centred * hid_centred, axis=-1, keepdims=True))
    normed = hid_centred * lax.rsqrt(hid_var + 1e-05)
    return jnp.dot(normed, occupancy_weight, precision=lax.Precision.HIGHEST, preferred_element_type=jnp.float32)

def reference(query, raw_flow_keys, flow_value_input, query_norm_gain, key_norm_gain, dec_keys, dec_values, block_ids, counts, page_of, point_weight, point_gain, occupancy_weight):
    flow_out = lax.map(lambda slot_item: flow_attention(slot_item[0], slot_item[1], slot_item[2], query_norm_gain, key_norm_gain), (query, raw_flow_keys, flow_value_input))
    slot_index = jnp.arange(SLOTS, dtype=jnp.int32)
    page_index = jnp.arange(PAGE_ROWS, dtype=jnp.int32)

    def shape_pages(slot_item):
        id_row, count_row, page_row, key_rows, value_rows = slot_item
        live_mask = slot_index % CAP < count_row[slot_index // CAP]
        page_match = (page_row[None, :] == page_index[:, None]) & live_mask[None, :]
        page_block = lax.optimization_barrier(jnp.sum(jnp.where(page_match, id_row[None, :], 0), axis=1)).astype(jnp.int32)
        present = jnp.any(page_match, axis=1)
        k_heads = jnp.transpose(key_rows.reshape(LATENT_TOKENS, DEC_HEADS, DEC_HEAD), (1, 0, 2))
        v_heads = jnp.transpose(value_rows.reshape(LATENT_TOKENS, DEC_HEADS, DEC_HEAD), (1, 0, 2))
        occ_rows = lax.map(lambda block_id: decode_block(block_id, k_heads, v_heads, point_weight, point_gain, occupancy_weight), page_block)
        return jnp.where(present[:, None], occ_rows, jnp.zeros_like(occ_rows))
    occupancy = lax.map(shape_pages, (block_ids, counts, page_of, dec_keys, dec_values))
    return (flow_out, occupancy)
```

```python
import math

import jax
import jax.numpy as jnp
from jax import lax
from jax.experimental import pallas as pl
from jax.experimental.pallas import tpu as pltpu
from jax.sharding import PartitionSpec as P

FLOW_HEAD_COUNT = 16
FLOW_HEAD_SIZE = 128
DEC_HEADS = 16
DEC_HEAD = 64
NFREQ = 8
RES = 512
SIDE = 8
PAGES = 1
QB = 512
PER_SIDE = 64


def norm_per_head(values_in, gain, head_count):
    flat_rows = values_in.shape[0]
    entries = values_in.astype(jnp.float32).reshape(flat_rows, head_count, -1)
    scaled = entries * lax.rsqrt(jnp.mean(entries * entries, axis=-1, keepdims=True) + 1e-06)
    return (scaled * gain).reshape(flat_rows, -1).astype(jnp.bfloat16)


def query_points(block_id):
    point_index = jnp.arange(QB, dtype=jnp.int32)
    cell_index = [
        block_id // (PER_SIDE * PER_SIDE) * SIDE + point_index // (SIDE * SIDE),
        block_id // PER_SIDE % PER_SIDE * SIDE + point_index // SIDE % SIDE,
        block_id % PER_SIDE * SIDE + point_index % SIDE,
    ]
    coords = jnp.stack(
        [(cell.astype(jnp.float32) + 0.5) * (2.0 / RES) - 1.0 for cell in cell_index], 0
    )
    frequency = math.pi * 2.0 ** jnp.arange(NFREQ).astype(jnp.float32)
    phases = (coords[:, None, :] * frequency[None, :, None]).reshape(3 * NFREQ, QB)
    return jnp.concatenate([coords, jnp.sin(phases), jnp.cos(phases)], 0)


def decode_block(block_id, k_heads, v_heads, point_weight, point_gain, occupancy_weight):
    features = query_points(block_id)
    start_proj = lax.dot_general(
        features,
        point_weight,
        (((0,), (0,)), ((), ())),
        precision=lax.Precision.HIGHEST,
        preferred_element_type=jnp.float32,
    )
    row_mean = jnp.mean(start_proj, axis=-1, keepdims=True)
    centred = start_proj - row_mean
    row_var = jnp.mean(centred * centred, axis=-1, keepdims=True)
    point_query = (centred * lax.rsqrt(row_var + 1e-05) * point_gain).astype(jnp.bfloat16)
    q_heads = jnp.transpose(point_query.reshape(QB, DEC_HEADS, DEC_HEAD), (1, 0, 2))

    def one_head(head_item):
        q_head, k_head, v_head = head_item
        score_matrix = jnp.dot(q_head, k_head.T, preferred_element_type=jnp.float32) / math.sqrt(
            DEC_HEAD
        )
        row_maximum = jnp.max(score_matrix, axis=-1, keepdims=True)
        weights = jnp.exp(score_matrix - row_maximum)
        row_sum = jnp.sum(weights, axis=-1, keepdims=True)
        mixed = jnp.dot(weights.astype(jnp.bfloat16), v_head, preferred_element_type=jnp.float32)
        return mixed / row_sum

    per_head = lax.map(one_head, (q_heads, k_heads, v_heads))
    hidden = start_proj + jnp.transpose(per_head, (1, 0, 2)).reshape(QB, -1)
    hid_mean = jnp.mean(hidden, axis=-1, keepdims=True)
    hid_centred = hidden - hid_mean
    hid_var = jnp.mean(hid_centred * hid_centred, axis=-1, keepdims=True)
    normed = hid_centred * lax.rsqrt(hid_var + 1e-05)
    return jnp.dot(
        normed,
        occupancy_weight,
        precision=lax.Precision.HIGHEST,
        preferred_element_type=jnp.float32,
    )


def decode_many(id_list, owner_list, k_all, value_all, point_weight, point_gain, occupancy_weight):

    def one_block(block_item):
        block_id, owner_shape = block_item
        k_heads = lax.dynamic_index_in_dim(k_all, owner_shape, 0, keepdims=False)
        v_heads = lax.dynamic_index_in_dim(value_all, owner_shape, 0, keepdims=False)
        return decode_block(block_id, k_heads, v_heads, point_weight, point_gain, occupancy_weight)

    return lax.map(one_block, (id_list, owner_list))


def body(
    query,
    raw_flow_keys,
    flow_value_input,
    query_norm_gain,
    key_norm_gain,
    dec_keys,
    dec_values,
    block_ids,
    counts,
    page_of,
    point_weight,
    point_gain,
    occupancy_weight,
):
    shape_number, token_rows, feature_width = query.shape
    scale_per_head = 1.0 / math.sqrt(FLOW_HEAD_SIZE)
    normed_queries = norm_per_head(
        query.reshape(shape_number * token_rows, feature_width), query_norm_gain, FLOW_HEAD_COUNT
    )
    normed_queries = normed_queries.reshape(shape_number, token_rows, feature_width)
    normed_keys = norm_per_head(
        raw_flow_keys.reshape(shape_number * token_rows, feature_width),
        key_norm_gain,
        FLOW_HEAD_COUNT,
    )
    normed_keys = normed_keys.reshape(shape_number, token_rows, feature_width)
    latents = (
        lax.all_gather(dec_keys, "block", axis=1, tiled=True),
        lax.all_gather(dec_values, "block", axis=1, tiled=True),
    )
    peer_total = lax.axis_size("block")
    query_split = normed_queries.reshape(shape_number, token_rows, FLOW_HEAD_COUNT, FLOW_HEAD_SIZE)
    row_maximum = jnp.full((shape_number, FLOW_HEAD_COUNT, token_rows), -1e30, jnp.float32)
    k_piece = lax.all_gather(normed_keys, "block", axis=1, tiled=True).reshape(
        shape_number, -1, FLOW_HEAD_COUNT, FLOW_HEAD_SIZE
    )
    v_piece = lax.all_gather(flow_value_input, "block", axis=1, tiled=True).reshape(
        shape_number, -1, FLOW_HEAD_COUNT, FLOW_HEAD_SIZE
    )
    score_matrix = (
        jnp.einsum("sqhe,skhe->shqk", query_split, k_piece, preferred_element_type=jnp.float32)
        * scale_per_head
    )
    new_max = jnp.maximum(row_maximum, jnp.max(score_matrix, axis=-1))
    weights = jnp.exp(score_matrix - new_max[..., None])
    row_sum = jnp.sum(weights, axis=-1)
    mixed_sum = jnp.einsum(
        "shqk,skhe->shqe", weights.astype(jnp.bfloat16), v_piece, preferred_element_type=jnp.float32
    )
    row_maximum, row_sum, mixed_sum = (new_max, row_sum, mixed_sum)
    attended = mixed_sum / row_sum[..., None]
    flow_out = (
        jnp.transpose(attended, (0, 2, 1, 3))
        .reshape(shape_number, token_rows, feature_width)
        .astype(jnp.bfloat16)
    )
    key_rows, value_rows = latents
    k_all = jnp.transpose(key_rows.reshape(shape_number, -1, DEC_HEADS, DEC_HEAD), (0, 2, 1, 3))
    value_all = jnp.transpose(
        value_rows.reshape(shape_number, -1, DEC_HEADS, DEC_HEAD), (0, 2, 1, 3)
    )
    slot_count = block_ids.shape[1]
    slot_index = jnp.arange(slot_count, dtype=jnp.int32)
    live_mask = slot_index[None, :] < counts
    dest_peer = page_of // PAGES
    local_page = page_of % PAGES
    peer_ids = jnp.arange(peer_total, dtype=jnp.int32)
    route = (dest_peer[:, None, :] == peer_ids[None, :, None]) & live_mask[:, None, :]
    page_tag = jnp.where(
        jnp.any(route, axis=-1), jnp.sum(jnp.where(route, local_page[:, None, :], 0), axis=-1), -1
    )
    page_tag = jnp.transpose(page_tag)
    page_range = jnp.arange(PAGES, dtype=jnp.int32)
    send_ids = jnp.transpose(jnp.sum(jnp.where(route, block_ids[:, None, :], 0), axis=-1))
    recv_ids, recv_tag = (
        lax.all_to_all(send_ids, "block", split_axis=0, concat_axis=0, tiled=True),
        lax.all_to_all(page_tag, "block", split_axis=0, concat_axis=0, tiled=True),
    )
    page_match = recv_tag[None, :, :] == page_range[:, None, None]
    chosen = jnp.sum(jnp.where(page_match, recv_ids[None, :, :], 0), axis=1)
    present = jnp.transpose(jnp.any(page_match, axis=1))
    owner_list = jnp.repeat(jnp.arange(shape_number, dtype=jnp.int32), PAGES)
    occ_rows = decode_many(
        jnp.transpose(chosen).reshape(-1),
        owner_list,
        k_all,
        value_all,
        point_weight,
        point_gain,
        occupancy_weight,
    )
    occ_rows = occ_rows.reshape(shape_number, PAGES, QB)
    occupancy = jnp.where(present[:, :, None], occ_rows, jnp.zeros_like(occ_rows))
    return (flow_out, occupancy)


F32, BF16 = jnp.float32, jnp.bfloat16
MESH_ID = pl.DeviceIdType.MESH
WIDTH = DEC_HEADS * DEC_HEAD
FEATS = 3 + 6 * NFREQ
ROWS = 64
GROUP = 4
GROUPS = DEC_HEADS // GROUP
GW = GROUP * DEC_HEAD
CAP = 4


def split(x):
    hi = x.astype(BF16)
    return hi, (x - hi.astype(F32)).astype(BF16)


def dot(a, b, ca, cb, precision=None):
    return lax.dot_general(
        a, b, (((ca,), (cb,)), ((), ())), precision=precision, preferred_element_type=F32
    )


def sine(r):
    r = ((r + 512) & 1023) - 512
    r = jnp.where(r > 256, 512 - r, jnp.where(r < -256, -512 - r, r))
    x = r.astype(F32) * (math.pi / 512)
    x2 = x * x
    acc = jnp.full_like(x, 1.0 / math.factorial(13))
    for order in (11, 9, 7, 5, 3, 1):
        sign = 1.0 if order % 4 == 1 else -1.0
        acc = acc * x2 + sign / math.factorial(order)
    return acc * x


def fused_kernel(
    n, q_in, k_in, v_in, qg_in, kg_in, dk_in, dv_in, id_in, cnt_in, page_in, pw_in, pg_in, ow_in,
    flow_out, occ_out,
    q_b, kv_b, dkv_b, int_b, cnt_b, gain_b, vec_b, pw_b,
    w_s, wg_s, gram_s, lt_s, ow_s, base_s, qhat_s, tok_s, kf_s, vf_s, hid_s,
    send_sem, recv_sem, local_sem, ready_sem,
):
    me = lax.axis_index("block")
    barrier = pltpu.get_barrier_semaphore()
    for peer in range(1, n):

        @pl.when(me < peer)
        def _():
            pl.semaphore_signal(barrier, inc=1, device_id={"block": peer}, device_id_type=MESH_ID)

    @pl.when(me > 0)
    def _():
        pl.semaphore_wait(barrier, me)

    moved = [
        (id_in, int_b, 0, 0), (page_in, int_b, 1, 0), (cnt_in, cnt_b, None, 1),
        (dk_in.at[0], dkv_b, 0, 2), (dv_in.at[0], dkv_b, 1, 2),
        (k_in.at[0], kv_b, 0, 3), (v_in.at[0], kv_b, 1, 3),
    ]

    def mine(buf, part):
        return buf.at[me] if part is None else buf.at[me, part]

    def send(peer):
        for src, buf, part, kind in moved:
            pltpu.make_async_remote_copy(
                src_ref=src, dst_ref=mine(buf, part),
                send_sem=send_sem.at[kind], recv_sem=recv_sem.at[kind],
                device_id={"block": peer}, device_id_type=MESH_ID,
            ).start()

    for peer in range(n - 1):

        @pl.when(me > peer)
        def _():
            pl.semaphore_signal(
                ready_sem.at[me - 1], inc=1, device_id={"block": peer}, device_id_type=MESH_ID
            )
            send(peer)

    plain = [
        (pw_in, pw_b, 0), (pg_in, vec_b.at[0], 1), (ow_in, vec_b.at[1], 1),
        (q_in.at[0], q_b, 2), (qg_in, gain_b.at[0], 3), (kg_in, gain_b.at[1], 3),
    ]
    for src, dst, kind in plain:
        pltpu.make_async_copy(src, dst, local_sem.at[kind]).start()
    for src, buf, part, kind in moved:
        pltpu.make_async_copy(src, mine(buf, part), recv_sem.at[kind]).start()

    def whole(ref, sem):
        pltpu.make_async_copy(ref, ref, sem).wait()

    whole(pw_b, local_sem.at[0])
    whole(vec_b, local_sem.at[1])
    whole(q_b, local_sem.at[2])
    whole(gain_b, local_sem.at[3])
    qg_b, kg_b, pg_b, ow_b = gain_b.at[0], gain_b.at[1], vec_b.at[0], vec_b.at[1]
    kinds = [int_b, cnt_b, dkv_b, kv_b]

    def arrive(kind):
        whole(kinds[kind], recv_sem.at[kind])

    w_s[...] = jnp.zeros_like(w_s)
    w_s[0:FEATS, :] = pw_b[...]
    w = w_s[...]
    centred = w - jnp.mean(w, axis=1, keepdims=True)
    gram_s[...] = dot(centred, centred, 1, 1, lax.Precision.HIGHEST) * (1.0 / WIDTH)
    wg_hi, wg_lo = split(centred * (pg_b[...] * (1.0 / math.sqrt(DEC_HEAD))))
    wg_s[0:ROWS, :] = wg_hi
    wg_s[ROWS : 2 * ROWS, :] = wg_hi
    wg_s[2 * ROWS : 3 * ROWS, :] = wg_lo
    wg_s[3 * ROWS :, :] = wg_lo
    w_hi = w.astype(BF16).astype(F32)
    w_lo = w - w_hi
    w_s[...] = w_lo
    lt_s[:, 0 : 2 * ROWS] = jnp.concatenate([w_hi, w_hi], 0).T.astype(BF16)
    ow_s[...] = jnp.broadcast_to(ow_b[...], (128, WIDTH)).T
    rho = lax.broadcasted_iota(jnp.int32, (ROWS, QB), 0)
    lane = lax.broadcasted_iota(jnp.int32, (ROWS, QB), 1)
    which = jnp.where(rho < 3 + 3 * NFREQ, rho - 3, rho - 3 - 3 * NFREQ)
    dim = jnp.where(rho < 3, rho, which >> 3)
    mult = jnp.where(rho < 3, 1, jnp.left_shift(1, which & 7))
    offset = jnp.where(dim == 0, lane >> 6, jnp.where(dim == 1, (lane >> 3) & 7, lane & 7))
    base_s[...] = (2 * offset + 1 - RES) * mult + jnp.where(rho >= 3 + 3 * NFREQ, RES // 2, 0)
    qhat_s[...] = jnp.zeros_like(qhat_s)
    for h in range(FLOW_HEAD_COUNT):
        cols = slice(h * FLOW_HEAD_SIZE, (h + 1) * FLOW_HEAD_SIZE)
        x = q_b[:, cols].astype(F32)
        x = x * lax.rsqrt(jnp.mean(x * x, axis=-1, keepdims=True) + 1e-06) * qg_b[...]
        qhat_s[0 : q_b.shape[0], cols] = x

    for peer in range(1, n):

        @pl.when(me < peer)
        def _():
            pl.semaphore_wait(ready_sem.at[peer - 1], 1)
            send(peer)

    arrive(0)
    arrive(1)
    slot = lax.broadcasted_iota(jnp.int32, (1, CAP), 1)
    found = jnp.zeros((1, CAP), F32)
    number = jnp.zeros((1, CAP), F32)
    for s in range(n):
        hit = (int_b[s, 1] == me) & (slot < cnt_b[s])
        found += jnp.where(hit, 1.0, 0.0)
        number += jnp.where(hit, int_b[s, 0].astype(F32), 0.0)
    present = jnp.sum(found, axis=1, keepdims=True) > 0.5
    block = jnp.sum(number, axis=1, keepdims=True).astype(jnp.int32)
    rows1 = lax.broadcasted_iota(jnp.int32, (ROWS, 128), 0)
    which1 = jnp.where(rows1 < 3 + 3 * NFREQ, rows1 - 3, rows1 - 3 - 3 * NFREQ)
    dim1 = jnp.where(rows1 < 3, rows1, which1 >> 3)
    mult1 = jnp.where(rows1 < 3, 1, jnp.left_shift(1, which1 & 7))
    cell = jnp.where(
        dim1 == 0, block >> 12, jnp.where(dim1 == 1, (block >> 6) & (PER_SIDE - 1), block & (PER_SIDE - 1))
    )
    cell = cell * mult1 * (2 * SIDE)
    r = base_s[...] + jnp.concatenate([cell] * (QB // 128), 1)
    feats = jnp.where(rho < 3, r.astype(F32) * (1.0 / RES), jnp.where(rho < FEATS, sine(r), 0.0))
    f_hi, f_lo = split(feats)
    f3 = jnp.concatenate([f_hi, f_lo, f_hi], 0)
    spread = dot(gram_s[...], feats, 1, 0, lax.Precision.HIGHEST)
    rstd = lax.rsqrt(jnp.sum(spread * feats, axis=0, keepdims=True) + 1e-05)

    per = q_b.shape[0]
    tokens = n * per
    rep_r = lax.broadcasted_iota(jnp.int32, (GROUP * tokens, tokens), 0)
    rep_c = lax.broadcasted_iota(jnp.int32, (GROUP * tokens, tokens), 1)
    repeat = jnp.where(rep_r // GROUP == rep_c, 1.0, 0.0).astype(BF16)
    head_r = lax.broadcasted_iota(jnp.int32, (GROUP * tokens, GW), 0)
    head_c = lax.broadcasted_iota(jnp.int32, (GROUP * tokens, GW), 1)
    own_head = head_r % GROUP == head_c // DEC_HEAD

    arrive(2)
    for s in range(n):
        tok_s[s * per : (s + 1) * per, :] = dkv_b[s, 0].astype(F32)
    key_rows = dot(repeat, tok_s[...].astype(BF16), 1, 0)
    probs = []
    for g in range(GROUPS):
        cols = slice(g * GW, (g + 1) * GW)
        kb = jnp.where(own_head, key_rows[:, cols], 0.0).astype(BF16)
        both = dot(kb, wg_s[:, cols], 1, 1)
        both = both[:, 0 : 2 * ROWS] + both[:, 2 * ROWS :]
        b_hi, b_lo = split(both)
        score = dot(jnp.concatenate([b_hi, b_lo[:, 0:ROWS]], 1), f3, 1, 0) * rstd
        score = score.reshape(-1, 8, QB)
        top = jnp.max(score, axis=0)
        top = jnp.maximum(top, pltpu.roll(top, 4, 0))
        e = jnp.exp(score - top[None])
        total = jnp.sum(e, axis=0)
        total = total + pltpu.roll(total, 4, 0)
        probs.append((e * (1.0 / total)[None]).reshape(GROUP * tokens, QB).astype(BF16))

    for s in range(n):
        tok_s[s * per : (s + 1) * per, :] = dkv_b[s, 1].astype(F32)
    value_rows = dot(repeat, tok_s[...].astype(BF16), 1, 0)
    mean = jnp.zeros((1, QB), F32)
    for g in range(GROUPS):
        cols = slice(g * GW, (g + 1) * GW)
        vb = jnp.where(own_head, value_rows[:, cols], 0.0)
        lt_s[cols, 2 * ROWS :] = jnp.concatenate([w_s[:, cols], vb], 0).T.astype(BF16)
        hid = dot(lt_s[cols, :], jnp.concatenate([f3, probs[g]], 0), 1, 0)
        hid_s[cols, :] = hid
        mean += jnp.sum(hid, axis=0, keepdims=True)
    mean = mean * (1.0 / WIDTH)
    var = jnp.zeros((1, QB), F32)
    logit = jnp.zeros((1, QB), F32)
    for g in range(GROUPS):
        cols = slice(g * GW, (g + 1) * GW)
        dev = hid_s[cols, :] - mean
        var += jnp.sum(dev * dev, axis=0, keepdims=True)
        ow = ow_s[cols, :]
        logit += jnp.sum(dev * jnp.concatenate([ow] * (QB // 128), 1), axis=0, keepdims=True)
    occ = logit * lax.rsqrt(var * (1.0 / WIDTH) + 1e-05)
    occ_out[0] = jnp.where(present, occ, 0.0)

    arrive(3)
    for s in range(n):
        kf_s[s * per : (s + 1) * per, :] = kv_b[s, 0].astype(F32)
    scores = []
    for h in range(FLOW_HEAD_COUNT):
        cols = slice(h * FLOW_HEAD_SIZE, (h + 1) * FLOW_HEAD_SIZE)
        x = kf_s[:, cols]
        x = x * lax.rsqrt(jnp.mean(x * x, axis=-1, keepdims=True) + 1e-06) * kg_b[...]
        scores.append(dot(qhat_s[:, cols].astype(BF16), x.astype(BF16), 1, 1)[0:8])
    score = jnp.concatenate(scores, 0) * (1.0 / math.sqrt(FLOW_HEAD_SIZE))
    weights = jnp.exp(score - jnp.max(score, axis=-1, keepdims=True))
    row_sum = jnp.sum(weights, axis=-1, keepdims=True)
    for s in range(n):
        vf_s[s * per : (s + 1) * per, :] = kv_b[s, 1].astype(F32)
    for h in range(FLOW_HEAD_COUNT):
        cols = slice(h * FLOW_HEAD_SIZE, (h + 1) * FLOW_HEAD_SIZE)
        rows = slice(h * 8, h * 8 + 8)
        mixed = dot(weights[rows].astype(BF16), vf_s[:, cols].astype(BF16), 1, 0)
        flow_out[0, :, cols] = (mixed / row_sum[rows])[0 : q_b.shape[0]].astype(BF16)

    for kind, buf in enumerate(kinds):
        whole(buf.at[0 : n - 1], send_sem.at[kind])


def write_out(flow_ref, occ_ref, flow_out, occ_out, sem):
    copies = [
        pltpu.make_async_copy(flow_ref, flow_out, sem.at[0]),
        pltpu.make_async_copy(occ_ref, occ_out, sem.at[1]),
    ]
    for copy in copies:
        copy.start()
    for copy in copies:
        copy.wait()


def fused_body(*args):
    (q, k, v, qg, kg, dk, dv, ids, counts, pages, pw, pg, ow) = args
    n = lax.axis_size("block")
    per = q.shape[1]
    tokens = n * per
    flow_width = q.shape[2]
    qg, kg, pg, ow = (x.reshape(1, -1) for x in (qg, kg, pg, ow))
    vmem = pltpu.VMEM
    made = pl.pallas_call(
        lambda *refs: fused_kernel(n, *refs),
        out_shape=(pltpu.VMEM(q.shape, BF16), pltpu.VMEM((1, PAGES, QB), F32)),
        in_specs=[pl.BlockSpec(memory_space=pltpu.HBM)] * 13,
        out_specs=(pl.BlockSpec(memory_space=pltpu.VMEM), pl.BlockSpec(memory_space=pltpu.VMEM)),
        scratch_shapes=[
            vmem((per, flow_width), BF16),
            vmem((n, 2, per, flow_width), BF16),
            vmem((n, 2, per, WIDTH), BF16),
            vmem((n, 2, 1, CAP), jnp.int32),
            vmem((n, 1, 1), jnp.int32),
            vmem((2, 1, FLOW_HEAD_SIZE), F32),
            vmem((2, 1, WIDTH), F32),
            vmem((FEATS, WIDTH), F32),
            vmem((ROWS, WIDTH), F32),
            vmem((4 * ROWS, WIDTH), BF16),
            vmem((ROWS, ROWS), F32),
            vmem((WIDTH, 4 * ROWS), BF16),
            vmem((WIDTH, 128), F32),
            vmem((ROWS, QB), jnp.int32),
            vmem((16, flow_width), F32),
            vmem((tokens, WIDTH), F32),
            vmem((tokens, flow_width), F32),
            vmem((tokens, flow_width), F32),
            vmem((WIDTH, QB), F32),
            pltpu.SemaphoreType.DMA((4,)),
            pltpu.SemaphoreType.DMA((4,)),
            pltpu.SemaphoreType.DMA((4,)),
            pltpu.SemaphoreType.REGULAR((n - 1,)),
        ],
        compiler_params=pltpu.CompilerParams(collective_id=0, has_side_effects=True),
    )(q, k, v, qg, kg, dk, dv, ids, counts, pages, pw, pg, ow)
    made = tuple(pltpu.with_memory_space_constraint(x, pltpu.VMEM) for x in made)
    return pl.pallas_call(
        write_out,
        out_shape=tuple(jax.ShapeDtypeStruct(x.shape, x.dtype) for x in made),
        in_specs=[pl.BlockSpec(memory_space=pltpu.VMEM)] * 2,
        out_specs=(pl.BlockSpec(memory_space=pltpu.HBM),) * 2,
        scratch_shapes=[pltpu.SemaphoreType.DMA((2,))],
    )(*made)


def solution(mesh):
    return jax.shard_map(
        fused_body if mesh.shape["block"] * 4 == 4 * GROUP else body,
        mesh=mesh,
        in_specs=(
            P(("groups", "shape"), "block", None),
            P(("groups", "shape"), "block", None),
            P(("groups", "shape"), "block", None),
            P(),
            P(),
            P(("groups", "shape"), "block", None),
            P(("groups", "shape"), "block", None),
            P(("groups", "shape"), "block"),
            P(("groups", "shape"), "block"),
            P(("groups", "shape"), "block"),
            P(),
            P(),
            P(),
        ),
        out_specs=(P(("groups", "shape"), "block", None), P(("groups", "shape"), "block", None)),
        check_vma=False,
    )
```

```python
import math

import jax
import jax.numpy as jnp
from jax import lax
from jax.experimental import pallas as pl
from jax.experimental.pallas import tpu as pltpu
from jax.sharding import PartitionSpec as P

FLOW_HEAD_COUNT = 16
FLOW_HEAD_SIZE = 128
DEC_HEADS = 16
DEC_HEAD = 64
NFREQ = 8
RES = 512
SIDE = 8
PAGES = 1
QB = 512
PER_SIDE = 64


def norm_per_head(values_in, gain, head_count):
    flat_rows = values_in.shape[0]
    entries = values_in.astype(jnp.float32).reshape(flat_rows, head_count, -1)
    scaled = entries * lax.rsqrt(jnp.mean(entries * entries, axis=-1, keepdims=True) + 1e-06)
    return (scaled * gain).reshape(flat_rows, -1).astype(jnp.bfloat16)


def query_points(block_id):
    point_index = jnp.arange(QB, dtype=jnp.int32)
    cell_index = [
        block_id // (PER_SIDE * PER_SIDE) * SIDE + point_index // (SIDE * SIDE),
        block_id // PER_SIDE % PER_SIDE * SIDE + point_index // SIDE % SIDE,
        block_id % PER_SIDE * SIDE + point_index % SIDE,
    ]
    coords = jnp.stack(
        [(cell.astype(jnp.float32) + 0.5) * (2.0 / RES) - 1.0 for cell in cell_index], 0
    )
    frequency = math.pi * 2.0 ** jnp.arange(NFREQ).astype(jnp.float32)
    phases = (coords[:, None, :] * frequency[None, :, None]).reshape(3 * NFREQ, QB)
    return jnp.concatenate([coords, jnp.sin(phases), jnp.cos(phases)], 0)


def decode_block(block_id, k_heads, v_heads, point_weight, point_gain, occupancy_weight):
    features = query_points(block_id)
    start_proj = lax.dot_general(
        features,
        point_weight,
        (((0,), (0,)), ((), ())),
        precision=lax.Precision.HIGHEST,
        preferred_element_type=jnp.float32,
    )
    row_mean = jnp.mean(start_proj, axis=-1, keepdims=True)
    centred = start_proj - row_mean
    row_var = jnp.mean(centred * centred, axis=-1, keepdims=True)
    point_query = (centred * lax.rsqrt(row_var + 1e-05) * point_gain).astype(jnp.bfloat16)
    q_heads = jnp.transpose(point_query.reshape(QB, DEC_HEADS, DEC_HEAD), (1, 0, 2))

    def one_head(head_item):
        q_head, k_head, v_head = head_item
        score_matrix = jnp.dot(q_head, k_head.T, preferred_element_type=jnp.float32) / math.sqrt(
            DEC_HEAD
        )
        row_maximum = jnp.max(score_matrix, axis=-1, keepdims=True)
        weights = jnp.exp(score_matrix - row_maximum)
        row_sum = jnp.sum(weights, axis=-1, keepdims=True)
        mixed = jnp.dot(weights.astype(jnp.bfloat16), v_head, preferred_element_type=jnp.float32)
        return mixed / row_sum

    per_head = lax.map(one_head, (q_heads, k_heads, v_heads))
    hidden = start_proj + jnp.transpose(per_head, (1, 0, 2)).reshape(QB, -1)
    hid_mean = jnp.mean(hidden, axis=-1, keepdims=True)
    hid_centred = hidden - hid_mean
    hid_var = jnp.mean(hid_centred * hid_centred, axis=-1, keepdims=True)
    normed = hid_centred * lax.rsqrt(hid_var + 1e-05)
    return jnp.dot(
        normed,
        occupancy_weight,
        precision=lax.Precision.HIGHEST,
        preferred_element_type=jnp.float32,
    )


def decode_many(id_list, owner_list, k_all, value_all, point_weight, point_gain, occupancy_weight):

    def one_block(block_item):
        block_id, owner_shape = block_item
        k_heads = lax.dynamic_index_in_dim(k_all, owner_shape, 0, keepdims=False)
        v_heads = lax.dynamic_index_in_dim(value_all, owner_shape, 0, keepdims=False)
        return decode_block(block_id, k_heads, v_heads, point_weight, point_gain, occupancy_weight)

    return lax.map(one_block, (id_list, owner_list))


def body(
    query,
    raw_flow_keys,
    flow_value_input,
    query_norm_gain,
    key_norm_gain,
    dec_keys,
    dec_values,
    block_ids,
    counts,
    page_of,
    point_weight,
    point_gain,
    occupancy_weight,
):
    shape_number, token_rows, feature_width = query.shape
    scale_per_head = 1.0 / math.sqrt(FLOW_HEAD_SIZE)
    normed_queries = norm_per_head(
        query.reshape(shape_number * token_rows, feature_width), query_norm_gain, FLOW_HEAD_COUNT
    )
    normed_queries = normed_queries.reshape(shape_number, token_rows, feature_width)
    normed_keys = norm_per_head(
        raw_flow_keys.reshape(shape_number * token_rows, feature_width),
        key_norm_gain,
        FLOW_HEAD_COUNT,
    )
    normed_keys = normed_keys.reshape(shape_number, token_rows, feature_width)
    latents = (
        lax.all_gather(dec_keys, "block", axis=1, tiled=True),
        lax.all_gather(dec_values, "block", axis=1, tiled=True),
    )
    peer_total = lax.axis_size("block")
    query_split = normed_queries.reshape(shape_number, token_rows, FLOW_HEAD_COUNT, FLOW_HEAD_SIZE)
    row_maximum = jnp.full((shape_number, FLOW_HEAD_COUNT, token_rows), -1e30, jnp.float32)
    k_piece = lax.all_gather(normed_keys, "block", axis=1, tiled=True).reshape(
        shape_number, -1, FLOW_HEAD_COUNT, FLOW_HEAD_SIZE
    )
    v_piece = lax.all_gather(flow_value_input, "block", axis=1, tiled=True).reshape(
        shape_number, -1, FLOW_HEAD_COUNT, FLOW_HEAD_SIZE
    )
    score_matrix = (
        jnp.einsum("sqhe,skhe->shqk", query_split, k_piece, preferred_element_type=jnp.float32)
        * scale_per_head
    )
    new_max = jnp.maximum(row_maximum, jnp.max(score_matrix, axis=-1))
    weights = jnp.exp(score_matrix - new_max[..., None])
    row_sum = jnp.sum(weights, axis=-1)
    mixed_sum = jnp.einsum(
        "shqk,skhe->shqe", weights.astype(jnp.bfloat16), v_piece, preferred_element_type=jnp.float32
    )
    row_maximum, row_sum, mixed_sum = (new_max, row_sum, mixed_sum)
    attended = mixed_sum / row_sum[..., None]
    flow_out = (
        jnp.transpose(attended, (0, 2, 1, 3))
        .reshape(shape_number, token_rows, feature_width)
        .astype(jnp.bfloat16)
    )
    key_rows, value_rows = latents
    k_all = jnp.transpose(key_rows.reshape(shape_number, -1, DEC_HEADS, DEC_HEAD), (0, 2, 1, 3))
    value_all = jnp.transpose(
        value_rows.reshape(shape_number, -1, DEC_HEADS, DEC_HEAD), (0, 2, 1, 3)
    )
    slot_count = block_ids.shape[1]
    slot_index = jnp.arange(slot_count, dtype=jnp.int32)
    live_mask = slot_index[None, :] < counts
    dest_peer = page_of // PAGES
    local_page = page_of % PAGES
    peer_ids = jnp.arange(peer_total, dtype=jnp.int32)
    route = (dest_peer[:, None, :] == peer_ids[None, :, None]) & live_mask[:, None, :]
    page_tag = jnp.where(
        jnp.any(route, axis=-1), jnp.sum(jnp.where(route, local_page[:, None, :], 0), axis=-1), -1
    )
    page_tag = jnp.transpose(page_tag)
    page_range = jnp.arange(PAGES, dtype=jnp.int32)
    send_ids = jnp.transpose(jnp.sum(jnp.where(route, block_ids[:, None, :], 0), axis=-1))
    recv_ids, recv_tag = (
        lax.all_to_all(send_ids, "block", split_axis=0, concat_axis=0, tiled=True),
        lax.all_to_all(page_tag, "block", split_axis=0, concat_axis=0, tiled=True),
    )
    page_match = recv_tag[None, :, :] == page_range[:, None, None]
    chosen = jnp.sum(jnp.where(page_match, recv_ids[None, :, :], 0), axis=1)
    present = jnp.transpose(jnp.any(page_match, axis=1))
    owner_list = jnp.repeat(jnp.arange(shape_number, dtype=jnp.int32), PAGES)
    occ_rows = decode_many(
        jnp.transpose(chosen).reshape(-1),
        owner_list,
        k_all,
        value_all,
        point_weight,
        point_gain,
        occupancy_weight,
    )
    occ_rows = occ_rows.reshape(shape_number, PAGES, QB)
    occupancy = jnp.where(present[:, :, None], occ_rows, jnp.zeros_like(occ_rows))
    return (flow_out, occupancy)


F32, BF16 = jnp.float32, jnp.bfloat16
MESH_ID = pl.DeviceIdType.MESH
WIDTH = DEC_HEADS * DEC_HEAD
FEATS = 3 + 6 * NFREQ
ROWS = 64
GROUP = 4
GROUPS = DEC_HEADS // GROUP
GW = GROUP * DEC_HEAD
CAP = 4


def split(x):
    hi = x.astype(BF16)
    return hi, (x - hi.astype(F32)).astype(BF16)


def dot(a, b, ca, cb, precision=None):
    return lax.dot_general(
        a, b, (((ca,), (cb,)), ((), ())), precision=precision, preferred_element_type=F32
    )


def sine(r):
    r = ((r + 512) & 1023) - 512
    r = jnp.where(r > 256, 512 - r, jnp.where(r < -256, -512 - r, r))
    x = r.astype(F32) * (math.pi / 512)
    x2 = x * x
    acc = jnp.full_like(x, 1.0 / math.factorial(13))
    for order in (11, 9, 7, 5, 3, 1):
        sign = 1.0 if order % 4 == 1 else -1.0
        acc = acc * x2 + sign / math.factorial(order)
    return acc * x


def fused_kernel(
    n, q_in, k_in, v_in, qg_in, kg_in, dk_in, dv_in, id_in, cnt_in, page_in, pw_in, pg_in, ow_in,
    flow_out, occ_out,
    q_b, kv_b, dkv_b, int_b, cnt_b, gain_b, vec_b, pw_b,
    w_s, wg_s, wx_s, gram_s, mid_s, near_s, far_s, qf_s, q_s, left_s, tok_s, kf_s, vf_s,
    send_sem, recv_sem, local_sem, ready_sem,
):
    me = lax.axis_index("block")
    barrier = pltpu.get_barrier_semaphore()
    for peer in range(1, n):

        @pl.when(me < peer)
        def _():
            pl.semaphore_signal(barrier, inc=1, device_id={"block": peer}, device_id_type=MESH_ID)

    @pl.when(me > 0)
    def _():
        pl.semaphore_wait(barrier, me)

    early = [
        (id_in, int_b, 0, 0), (page_in, int_b, 1, 0), (cnt_in, cnt_b, None, 1),
        (dk_in.at[0], dkv_b, 0, 3), (dv_in.at[0], dkv_b, 1, 3),
    ]
    late = [(k_in.at[0], kv_b, 0, 2), (v_in.at[0], kv_b, 1, 2)]

    def mine(buf, part):
        return buf.at[me] if part is None else buf.at[me, part]

    def send(peer, moved):
        final = n - 1 if 2 * peer < n else 0
        for src, buf, part, kind in moved:
            into = kind
            if kind == 3:
                into = jnp.where(me == final, 5, jnp.where(me == peer - 1, 4, 3))
            pltpu.make_async_remote_copy(
                src_ref=src, dst_ref=mine(buf, part),
                send_sem=send_sem.at[kind], recv_sem=recv_sem.at[into],
                device_id={"block": peer}, device_id_type=MESH_ID,
            ).start()

    for peer in range(n - 1):

        @pl.when(me > peer)
        def _():
            pl.semaphore_signal(
                ready_sem.at[me - 1], inc=1, device_id={"block": peer}, device_id_type=MESH_ID
            )
            send(peer, early)
            if peer == 0:
                send(peer, late)

    plain = [
        (pw_in, pw_b, 0), (pg_in, vec_b.at[0], 1), (ow_in, vec_b.at[1], 1),
        (q_in.at[0], q_b, 2), (qg_in, gain_b.at[0], 3), (kg_in, gain_b.at[1], 3),
    ]
    for src, dst, kind in plain:
        pltpu.make_async_copy(src, dst, local_sem.at[kind]).start()
    for src, buf, part, kind in early + late:
        pltpu.make_async_copy(src, mine(buf, part), recv_sem.at[kind]).start()

    def whole(ref, sem):
        pltpu.make_async_copy(ref, ref, sem).wait()

    whole(pw_b, local_sem.at[0])
    whole(vec_b, local_sem.at[1])
    whole(q_b, local_sem.at[2])
    whole(gain_b, local_sem.at[3])
    kinds = [int_b, cnt_b, kv_b, dkv_b]

    def arrive(kind):
        whole(kinds[kind], recv_sem.at[kind])

    w_s[...] = jnp.zeros_like(w_s)
    w_s[0:FEATS, :] = pw_b[...]
    w = w_s[...]
    centred = w - jnp.mean(w, axis=1, keepdims=True)
    ow = vec_b[1]
    twice = jnp.concatenate([centred, centred], 0)
    gram = dot(
        jnp.concatenate([centred, jnp.broadcast_to(ow * WIDTH, (16, WIDTH))], 0),
        twice, 1, 1, lax.Precision.HIGHEST,
    ) * (1.0 / WIDTH)
    g_hi, g_lo = split(gram)
    gram_s[...] = jnp.concatenate([g_hi, g_lo[:, 0:ROWS]], 1)
    for ref, values in ((wg_s, centred * (vec_b[0] * (1.0 / math.sqrt(DEC_HEAD)))), (wx_s, centred * 2.0)):
        hi, lo = split(values)
        ref[0:ROWS, :] = hi
        ref[ROWS:, :] = lo
    o_hi, o_lo = split(ow - jnp.mean(ow, axis=1, keepdims=True))
    line = lax.broadcasted_iota(jnp.int32, (16, WIDTH), 0)
    mid = jnp.where(line == 0, o_hi.astype(F32), jnp.where(line == 1, o_lo.astype(F32), 0.0))
    mid_s[...] = jnp.where(line == 2, 1.0 / WIDTH, mid).astype(BF16)

    rho = lax.broadcasted_iota(jnp.int32, (ROWS, QB), 0)
    lane = lax.broadcasted_iota(jnp.int32, (ROWS, QB), 1)
    which = jnp.where(rho < 3 + 3 * NFREQ, rho - 3, rho - 3 - 3 * NFREQ)
    dim = jnp.where(rho < 3, rho, which >> 3)
    mult = jnp.where(rho < 3, 1, jnp.left_shift(1, which & 7))
    offset = jnp.where(dim == 0, lane >> 6, jnp.where(dim == 1, (lane >> 3) & 7, lane & 7))
    base = (2 * offset + 1 - RES) * mult + jnp.where(rho >= 3 + 3 * NFREQ, RES // 2, 0)
    near_s[...] = jnp.where(rho < 3, base.astype(F32) * (1.0 / RES), jnp.where(rho < FEATS, sine(base), 0.0))
    far_s[...] = jnp.where(rho < 3, 1.0, jnp.where(rho < FEATS, sine(base + RES // 2), 0.0))

    per = q_b.shape[0]
    tokens = n * per
    qf_s[...] = jnp.zeros_like(qf_s)
    for h in range(FLOW_HEAD_COUNT):
        cols = slice(h * FLOW_HEAD_SIZE, (h + 1) * FLOW_HEAD_SIZE)
        x = q_b[:, cols].astype(F32)
        x = x * lax.rsqrt(jnp.mean(x * x, axis=-1, keepdims=True) + 1e-06) * (gain_b[0] * gain_b[1])
        qf_s[h * per : (h + 1) * per, cols] = x
    half = FLOW_HEAD_COUNT * per
    q_s[:, 0:half] = qf_s[...].T.astype(BF16)
    pick_r = lax.broadcasted_iota(jnp.int32, (q_s.shape[0], half), 0)
    pick_c = lax.broadcasted_iota(jnp.int32, (q_s.shape[0], half), 1)
    q_s[:, half:] = jnp.where(pick_c // per == pick_r // FLOW_HEAD_SIZE, 1.0, 0.0).astype(BF16)

    for peer in range(1, n - 1):

        @pl.when(me > peer)
        def _():
            send(peer, late)

    for peer in range(1, n):

        @pl.when(me < peer)
        def _():
            pl.semaphore_wait(ready_sem.at[peer - 1], 1)
            send(peer, early)

    @pl.when(me == 0)
    def _():
        for peer in range(1, n):
            send(peer, late)
        whole(dkv_b.at[0 : n - 1], recv_sem.at[3])

    @pl.when(me > 0)
    def _():
        whole(dkv_b.at[0], recv_sem.at[4])

    for peer in range(2, n):

        @pl.when((me > 0) & (me < peer))
        def _():
            send(peer, late)

    @pl.when(me > 0)
    def _():
        whole(dkv_b.at[0 : n - 2], recv_sem.at[3])

    shift = jnp.where(2 * me < n, 0, 1)
    final = (n - 1) * (1 - shift)

    def place(row, source):
        for part in range(2):
            x = dkv_b[source, part].astype(F32)
            for c in range(WIDTH // 128):
                for twin in range(2):
                    tok_s[part * (WIDTH // 128) + c, pl.ds(2 * per * row + twin, per, stride=2), :] = x[
                        :, c * 128 : (c + 1) * 128
                    ]

    for row in range(n - 1):
        place(row, row + shift)
    arrive(0)
    arrive(1)
    whole(dkv_b.at[0], recv_sem.at[5])
    place(n - 1, final)
    rows_g = GROUP * tokens
    head_r = lax.broadcasted_iota(jnp.int32, (2, 2 * per, GW), 0) * 2
    head_r += lax.broadcasted_iota(jnp.int32, (2, 2 * per, GW), 1) & 1
    own_head = head_r == lax.broadcasted_iota(jnp.int32, (2, 2 * per, GW), 2) // DEC_HEAD

    def blocks(first):
        x = jnp.concatenate([tok_s[first // 128 + i] for i in range(GW // 128)], 1)
        x = x.reshape(n, 1, 2 * per, GW)
        return jnp.where(own_head[None], x, 0.0).reshape(rows_g, GW).astype(BF16)

    shape = (rows_g + 16, 2 * ROWS)
    low_row = lax.broadcasted_iota(jnp.int32, shape, 0) < rows_g
    left = []
    for g in range(GROUPS):
        cols = slice(g * GW, (g + 1) * GW)
        b = dot(blocks(g * GW), wg_s[:, cols], 1, 1)
        b_hi, b_lo = split(b + pltpu.roll(b, ROWS, 1))
        left.append(jnp.concatenate([b_hi, b_lo[:, 0:ROWS]], 1))
        vb = blocks(WIDTH + g * GW)
        both = dot(jnp.concatenate([vb, mid_s[:, cols]], 0), jnp.concatenate([wx_s[:, cols], vb], 0), 1, 1)
        x = both[:, 0 : 2 * ROWS]
        x = jnp.where(low_row, x + pltpu.roll(x, ROWS, 1), 0.0)
        y = both[:, 2 * ROWS :]
        x_hi = x.astype(BF16)
        y_hi = y.astype(BF16)
        left_s[g, :, 0 : 2 * ROWS] = x_hi
        left_s[g, :, 2 * ROWS : 3 * ROWS] = y_hi
        left_s[g, :, 3 * ROWS : 4 * ROWS] = (x - x_hi.astype(F32)).astype(BF16)[:, ROWS:]
        left_s[g, :, 4 * ROWS :] = (y - y_hi.astype(F32)).astype(BF16)

    slot = lax.broadcasted_iota(jnp.int32, (1, CAP), 1)
    number = jnp.zeros((1, CAP), F32)
    for s in range(n):
        hit = (int_b[s, 1] == me) & (slot < cnt_b[s])
        number += jnp.where(hit, (int_b[s, 0] + 1).astype(F32), 0.0)
    number = jnp.sum(number, axis=1, keepdims=True)
    present = number > 0.5
    block = jnp.maximum(number - 1.0, 0.0).astype(jnp.int32)
    rows1 = lax.broadcasted_iota(jnp.int32, (ROWS, 128), 0)
    which1 = jnp.where(rows1 < 3 + 3 * NFREQ, rows1 - 3, rows1 - 3 - 3 * NFREQ)
    dim1 = jnp.where(rows1 < 3, rows1, which1 >> 3)
    mult1 = jnp.where(rows1 < 3, 1, jnp.left_shift(1, which1 & 7))
    cell = jnp.where(
        dim1 == 0, block >> 12, jnp.where(dim1 == 1, (block >> 6) & (PER_SIDE - 1), block & (PER_SIDE - 1))
    )
    cell = cell * mult1 * (2 * SIDE)
    turn = jnp.where(rows1 < 3, 1.0, sine(cell + RES // 2))
    step = jnp.where(rows1 < 3, cell.astype(F32) * (1.0 / RES), sine(cell))
    feats = near_s[...] * jnp.concatenate([turn] * (QB // 128), 1)
    feats += far_s[...] * jnp.concatenate([step] * (QB // 128), 1)
    f_hi, f_lo = split(feats)
    f3 = jnp.concatenate([f_hi, f_lo, f_hi], 0)

    scores = dot(jnp.concatenate(left + [gram_s[...]], 0), f3, 1, 0)
    below = GROUPS * rows_g
    spread = jnp.sum(scores[below : below + ROWS] * feats, axis=0, keepdims=True)
    logit = scores[below + ROWS : below + ROWS + 1]
    rstd = lax.rsqrt(spread + 1e-05)

    squares = jnp.zeros((8, QB), F32)
    linear = jnp.zeros((8, QB), F32)
    for g in range(GROUPS):
        score = scores[g * rows_g : (g + 1) * rows_g] * rstd
        score = score.reshape(n, 2, 2 * per, QB)
        top = jnp.max(score, axis=0)
        top = jnp.maximum(top, pltpu.roll(top, 4, 1))
        top = jnp.maximum(top, pltpu.roll(top, 2, 1))
        e = jnp.exp(score - top[None])
        total = jnp.sum(e, axis=0)
        total = total + pltpu.roll(total, 4, 1)
        total = total + pltpu.roll(total, 2, 1)
        probs = (e * (1.0 / total)[None]).reshape(rows_g, QB).astype(BF16)
        out = dot(left_s[g], jnp.concatenate([f_hi, f_lo, probs, f_hi, probs], 0), 1, 0)
        squares += jnp.sum((out[0:rows_g] * probs.astype(F32)).reshape(-1, 8, QB), axis=0)
        linear += out[rows_g : rows_g + 8]
    mean = linear[2:3]
    logit += linear[0:1] + linear[1:2]
    var = spread + jnp.sum(squares, axis=0, keepdims=True) * (1.0 / WIDTH) - mean * mean
    occ = logit * lax.rsqrt(jnp.maximum(var, 0.0) + 1e-05)
    occ_out[0] = jnp.where(present, occ, 0.0)

    arrive(2)
    for s in range(n):
        kf_s[s * per : (s + 1) * per, :] = kv_b[s, 0].astype(F32)
        vf_s[s * per : (s + 1) * per, :] = kv_b[s, 1].astype(F32)
    keys = kf_s[...]
    s_hi, s_lo = split(keys * keys)
    both = dot(jnp.concatenate([keys.astype(BF16), s_hi, s_lo], 0), q_s[...], 1, 0)
    size = pltpu.roll(both[tokens : 2 * tokens] + both[2 * tokens :], half, 1)
    size = lax.rsqrt(size * (1.0 / FLOW_HEAD_SIZE) + 1e-06) * (1.0 / math.sqrt(FLOW_HEAD_SIZE))
    score = both[0:tokens] * size
    weights = jnp.exp(score - jnp.max(score, axis=0, keepdims=True))
    inverse = jnp.broadcast_to(1.0 / jnp.sum(weights, axis=0, keepdims=True), (8, 2 * half))
    turned = jnp.concatenate([weights, inverse], 0).T
    for r in range(FLOW_HEAD_COUNT // 2):
        cols = slice(2 * r * FLOW_HEAD_SIZE, 2 * (r + 1) * FLOW_HEAD_SIZE)
        rows = turned[2 * r * per : 2 * (r + 1) * per]
        mixed = dot(rows[:, 0:tokens].astype(BF16), vf_s[:, cols].astype(BF16), 1, 0)
        mixed = mixed * rows[:, tokens : tokens + 1]
        mixed = jnp.concatenate([mixed[0:per, 0:FLOW_HEAD_SIZE], mixed[per:, FLOW_HEAD_SIZE:]], 1)
        flow_out[0, :, cols] = mixed.astype(BF16)

    for kind, buf in enumerate(kinds):
        whole(buf.at[0 : n - 1], send_sem.at[kind])


def write_out(flow_ref, occ_ref, flow_out, occ_out, sem):
    copies = [
        pltpu.make_async_copy(flow_ref, flow_out, sem.at[0]),
        pltpu.make_async_copy(occ_ref, occ_out, sem.at[1]),
    ]
    for copy in copies:
        copy.start()
    for copy in copies:
        copy.wait()


def fused_body(*args):
    (q, k, v, qg, kg, dk, dv, ids, counts, pages, pw, pg, ow) = args
    n = lax.axis_size("block")
    per = q.shape[1]
    tokens = n * per
    flow_width = q.shape[2]
    qg, kg, pg, ow = (x.reshape(1, -1) for x in (qg, kg, pg, ow))
    vmem = pltpu.VMEM
    made = pl.pallas_call(
        lambda *refs: fused_kernel(n, *refs),
        out_shape=(pltpu.VMEM(q.shape, BF16), pltpu.VMEM((1, PAGES, QB), F32)),
        in_specs=[pl.BlockSpec(memory_space=pltpu.HBM)] * 13,
        out_specs=(pl.BlockSpec(memory_space=pltpu.VMEM), pl.BlockSpec(memory_space=pltpu.VMEM)),
        scratch_shapes=[
            vmem((per, flow_width), BF16),
            vmem((n, 2, per, flow_width), BF16),
            vmem((n, 2, per, WIDTH), BF16),
            vmem((n, 2, 1, CAP), jnp.int32),
            vmem((n, 1, 1), jnp.int32),
            vmem((2, 1, FLOW_HEAD_SIZE), F32),
            vmem((2, 1, WIDTH), F32),
            vmem((FEATS, WIDTH), F32),
            vmem((ROWS, WIDTH), F32),
            vmem((2 * ROWS, WIDTH), BF16),
            vmem((2 * ROWS, WIDTH), BF16),
            vmem((ROWS + 16, 3 * ROWS), BF16),
            vmem((16, WIDTH), BF16),
            vmem((ROWS, QB), F32),
            vmem((ROWS, QB), F32),
            vmem((FLOW_HEAD_COUNT * per, flow_width), F32),
            vmem((flow_width, 2 * FLOW_HEAD_COUNT * per), BF16),
            vmem((GROUPS, GROUP * tokens + 16, 5 * ROWS), BF16),
            vmem((2 * WIDTH // 128, 2 * tokens, 128), F32),
            vmem((tokens, flow_width), F32),
            vmem((tokens, flow_width), F32),
            pltpu.SemaphoreType.DMA((4,)),
            pltpu.SemaphoreType.DMA((6,)),
            pltpu.SemaphoreType.DMA((4,)),
            pltpu.SemaphoreType.REGULAR((n - 1,)),
        ],
        compiler_params=pltpu.CompilerParams(collective_id=0, has_side_effects=True),
    )(q, k, v, qg, kg, dk, dv, ids, counts, pages, pw, pg, ow)
    made = tuple(pltpu.with_memory_space_constraint(x, pltpu.VMEM) for x in made)
    return pl.pallas_call(
        write_out,
        out_shape=tuple(jax.ShapeDtypeStruct(x.shape, x.dtype) for x in made),
        in_specs=[pl.BlockSpec(memory_space=pltpu.VMEM)] * 2,
        out_specs=(pl.BlockSpec(memory_space=pltpu.HBM),) * 2,
        scratch_shapes=[pltpu.SemaphoreType.DMA((2,))],
    )(*made)


def solution(mesh):
    return jax.shard_map(
        fused_body if mesh.shape["block"] * 4 == 4 * GROUP else body,
        mesh=mesh,
        in_specs=(
            P(("groups", "shape"), "block", None),
            P(("groups", "shape"), "block", None),
            P(("groups", "shape"), "block", None),
            P(),
            P(),
            P(("groups", "shape"), "block", None),
            P(("groups", "shape"), "block", None),
            P(("groups", "shape"), "block"),
            P(("groups", "shape"), "block"),
            P(("groups", "shape"), "block"),
            P(),
            P(),
            P(),
        ),
        out_specs=(P(("groups", "shape"), "block", None), P(("groups", "shape"), "block", None)),
        check_vma=False,
    )
```

```python
import math

import jax
import jax.numpy as jnp
from jax import lax
from jax.experimental import pallas as pl
from jax.experimental.pallas import tpu as pltpu
from jax.sharding import PartitionSpec as P

FLOW_HEAD_COUNT = 16
FLOW_HEAD_SIZE = 128
DEC_HEADS = 16
DEC_HEAD = 64
NFREQ = 8
RES = 512
SIDE = 8
PAGES = 1
QB = 512
PER_SIDE = 64


def norm_per_head(values_in, gain, head_count):
    flat_rows = values_in.shape[0]
    entries = values_in.astype(jnp.float32).reshape(flat_rows, head_count, -1)
    scaled = entries * lax.rsqrt(jnp.mean(entries * entries, axis=-1, keepdims=True) + 1e-06)
    return (scaled * gain).reshape(flat_rows, -1).astype(jnp.bfloat16)


def query_points(block_id):
    point_index = jnp.arange(QB, dtype=jnp.int32)
    cell_index = [
        block_id // (PER_SIDE * PER_SIDE) * SIDE + point_index // (SIDE * SIDE),
        block_id // PER_SIDE % PER_SIDE * SIDE + point_index // SIDE % SIDE,
        block_id % PER_SIDE * SIDE + point_index % SIDE,
    ]
    coords = jnp.stack(
        [(cell.astype(jnp.float32) + 0.5) * (2.0 / RES) - 1.0 for cell in cell_index], 0
    )
    frequency = math.pi * 2.0 ** jnp.arange(NFREQ).astype(jnp.float32)
    phases = (coords[:, None, :] * frequency[None, :, None]).reshape(3 * NFREQ, QB)
    return jnp.concatenate([coords, jnp.sin(phases), jnp.cos(phases)], 0)


def decode_block(block_id, k_heads, v_heads, point_weight, point_gain, occupancy_weight):
    features = query_points(block_id)
    start_proj = lax.dot_general(
        features,
        point_weight,
        (((0,), (0,)), ((), ())),
        precision=lax.Precision.HIGHEST,
        preferred_element_type=jnp.float32,
    )
    row_mean = jnp.mean(start_proj, axis=-1, keepdims=True)
    centred = start_proj - row_mean
    row_var = jnp.mean(centred * centred, axis=-1, keepdims=True)
    point_query = (centred * lax.rsqrt(row_var + 1e-05) * point_gain).astype(jnp.bfloat16)
    q_heads = jnp.transpose(point_query.reshape(QB, DEC_HEADS, DEC_HEAD), (1, 0, 2))

    def one_head(head_item):
        q_head, k_head, v_head = head_item
        score_matrix = jnp.dot(q_head, k_head.T, preferred_element_type=jnp.float32) / math.sqrt(
            DEC_HEAD
        )
        row_maximum = jnp.max(score_matrix, axis=-1, keepdims=True)
        weights = jnp.exp(score_matrix - row_maximum)
        row_sum = jnp.sum(weights, axis=-1, keepdims=True)
        mixed = jnp.dot(weights.astype(jnp.bfloat16), v_head, preferred_element_type=jnp.float32)
        return mixed / row_sum

    per_head = lax.map(one_head, (q_heads, k_heads, v_heads))
    hidden = start_proj + jnp.transpose(per_head, (1, 0, 2)).reshape(QB, -1)
    hid_mean = jnp.mean(hidden, axis=-1, keepdims=True)
    hid_centred = hidden - hid_mean
    hid_var = jnp.mean(hid_centred * hid_centred, axis=-1, keepdims=True)
    normed = hid_centred * lax.rsqrt(hid_var + 1e-05)
    return jnp.dot(
        normed,
        occupancy_weight,
        precision=lax.Precision.HIGHEST,
        preferred_element_type=jnp.float32,
    )


def decode_many(id_list, owner_list, k_all, value_all, point_weight, point_gain, occupancy_weight):

    def one_block(block_item):
        block_id, owner_shape = block_item
        k_heads = lax.dynamic_index_in_dim(k_all, owner_shape, 0, keepdims=False)
        v_heads = lax.dynamic_index_in_dim(value_all, owner_shape, 0, keepdims=False)
        return decode_block(block_id, k_heads, v_heads, point_weight, point_gain, occupancy_weight)

    return lax.map(one_block, (id_list, owner_list))


def body(
    query,
    raw_flow_keys,
    flow_value_input,
    query_norm_gain,
    key_norm_gain,
    dec_keys,
    dec_values,
    block_ids,
    counts,
    page_of,
    point_weight,
    point_gain,
    occupancy_weight,
):
    shape_number, token_rows, feature_width = query.shape
    scale_per_head = 1.0 / math.sqrt(FLOW_HEAD_SIZE)
    normed_queries = norm_per_head(
        query.reshape(shape_number * token_rows, feature_width), query_norm_gain, FLOW_HEAD_COUNT
    )
    normed_queries = normed_queries.reshape(shape_number, token_rows, feature_width)
    normed_keys = norm_per_head(
        raw_flow_keys.reshape(shape_number * token_rows, feature_width),
        key_norm_gain,
        FLOW_HEAD_COUNT,
    )
    normed_keys = normed_keys.reshape(shape_number, token_rows, feature_width)
    latents = (
        lax.all_gather(dec_keys, "block", axis=1, tiled=True),
        lax.all_gather(dec_values, "block", axis=1, tiled=True),
    )
    peer_total = lax.axis_size("block")
    query_split = normed_queries.reshape(shape_number, token_rows, FLOW_HEAD_COUNT, FLOW_HEAD_SIZE)
    row_maximum = jnp.full((shape_number, FLOW_HEAD_COUNT, token_rows), -1e30, jnp.float32)
    k_piece = lax.all_gather(normed_keys, "block", axis=1, tiled=True).reshape(
        shape_number, -1, FLOW_HEAD_COUNT, FLOW_HEAD_SIZE
    )
    v_piece = lax.all_gather(flow_value_input, "block", axis=1, tiled=True).reshape(
        shape_number, -1, FLOW_HEAD_COUNT, FLOW_HEAD_SIZE
    )
    score_matrix = (
        jnp.einsum("sqhe,skhe->shqk", query_split, k_piece, preferred_element_type=jnp.float32)
        * scale_per_head
    )
    new_max = jnp.maximum(row_maximum, jnp.max(score_matrix, axis=-1))
    weights = jnp.exp(score_matrix - new_max[..., None])
    row_sum = jnp.sum(weights, axis=-1)
    mixed_sum = jnp.einsum(
        "shqk,skhe->shqe", weights.astype(jnp.bfloat16), v_piece, preferred_element_type=jnp.float32
    )
    row_maximum, row_sum, mixed_sum = (new_max, row_sum, mixed_sum)
    attended = mixed_sum / row_sum[..., None]
    flow_out = (
        jnp.transpose(attended, (0, 2, 1, 3))
        .reshape(shape_number, token_rows, feature_width)
        .astype(jnp.bfloat16)
    )
    key_rows, value_rows = latents
    k_all = jnp.transpose(key_rows.reshape(shape_number, -1, DEC_HEADS, DEC_HEAD), (0, 2, 1, 3))
    value_all = jnp.transpose(
        value_rows.reshape(shape_number, -1, DEC_HEADS, DEC_HEAD), (0, 2, 1, 3)
    )
    slot_count = block_ids.shape[1]
    slot_index = jnp.arange(slot_count, dtype=jnp.int32)
    live_mask = slot_index[None, :] < counts
    dest_peer = page_of // PAGES
    local_page = page_of % PAGES
    peer_ids = jnp.arange(peer_total, dtype=jnp.int32)
    route = (dest_peer[:, None, :] == peer_ids[None, :, None]) & live_mask[:, None, :]
    page_tag = jnp.where(
        jnp.any(route, axis=-1), jnp.sum(jnp.where(route, local_page[:, None, :], 0), axis=-1), -1
    )
    page_tag = jnp.transpose(page_tag)
    page_range = jnp.arange(PAGES, dtype=jnp.int32)
    send_ids = jnp.transpose(jnp.sum(jnp.where(route, block_ids[:, None, :], 0), axis=-1))
    recv_ids, recv_tag = (
        lax.all_to_all(send_ids, "block", split_axis=0, concat_axis=0, tiled=True),
        lax.all_to_all(page_tag, "block", split_axis=0, concat_axis=0, tiled=True),
    )
    page_match = recv_tag[None, :, :] == page_range[:, None, None]
    chosen = jnp.sum(jnp.where(page_match, recv_ids[None, :, :], 0), axis=1)
    present = jnp.transpose(jnp.any(page_match, axis=1))
    owner_list = jnp.repeat(jnp.arange(shape_number, dtype=jnp.int32), PAGES)
    occ_rows = decode_many(
        jnp.transpose(chosen).reshape(-1),
        owner_list,
        k_all,
        value_all,
        point_weight,
        point_gain,
        occupancy_weight,
    )
    occ_rows = occ_rows.reshape(shape_number, PAGES, QB)
    occupancy = jnp.where(present[:, :, None], occ_rows, jnp.zeros_like(occ_rows))
    return (flow_out, occupancy)


F32, BF16 = jnp.float32, jnp.bfloat16
MESH_ID = pl.DeviceIdType.MESH
WIDTH = DEC_HEADS * DEC_HEAD
FEATS = 3 + 6 * NFREQ
ROWS = 64
GROUP = 4
GROUPS = DEC_HEADS // GROUP
GW = GROUP * DEC_HEAD
CAP = 4


def split(x):
    hi = x.astype(BF16)
    return hi, (x - hi.astype(F32)).astype(BF16)


def dot(a, b, ca, cb, precision=None):
    return lax.dot_general(
        a, b, (((ca,), (cb,)), ((), ())), precision=precision, preferred_element_type=F32
    )


def sine(r):
    r = ((r + 512) & 1023) - 512
    r = jnp.where(r > 256, 512 - r, jnp.where(r < -256, -512 - r, r))
    x = r.astype(F32) * (math.pi / 512)
    x2 = x * x
    acc = jnp.full_like(x, 1.0 / math.factorial(13))
    for order in (11, 9, 7, 5, 3, 1):
        sign = 1.0 if order % 4 == 1 else -1.0
        acc = acc * x2 + sign / math.factorial(order)
    return acc * x


def fused_kernel(
    n, q_in, k_in, v_in, qg_in, kg_in, dk_in, dv_in, id_in, cnt_in, page_in, pw_in, pg_in, ow_in,
    flow_out, occ_out,
    q_b, kv_b, dkv_b, int_b, cnt_b, gain_b, vec_b, pw_b,
    w_s, wg_s, wx_s, gram_s, mid_s, near_s, far_s, qf_s, q_s, form_s, tok_s, kf_s, vf_s,
    send_sem, recv_sem, local_sem, ready_sem,
):
    me = lax.axis_index("block")
    barrier = pltpu.get_barrier_semaphore()
    for peer in range(1, n):

        @pl.when(me < peer)
        def _():
            pl.semaphore_signal(barrier, inc=1, device_id={"block": peer}, device_id_type=MESH_ID)

    @pl.when(me > 0)
    def _():
        pl.semaphore_wait(barrier, me)

    early = [
        (id_in, int_b, 0, 0), (page_in, int_b, 1, 0), (cnt_in, cnt_b, None, 1),
        (dk_in.at[0], dkv_b, 0, 3), (dv_in.at[0], dkv_b, 1, 3),
    ]
    late = [(k_in.at[0], kv_b, 0, 2), (v_in.at[0], kv_b, 1, 2)]

    def mine(buf, part):
        return buf.at[me] if part is None else buf.at[me, part]

    def send(peer, moved):
        final = n - 1 if 2 * peer < n else 0
        for src, buf, part, kind in moved:
            into = kind
            if kind == 3:
                into = jnp.where(me == final, 5, jnp.where(me == peer - 1, 4, 3))
            pltpu.make_async_remote_copy(
                src_ref=src, dst_ref=mine(buf, part),
                send_sem=send_sem.at[kind], recv_sem=recv_sem.at[into],
                device_id={"block": peer}, device_id_type=MESH_ID,
            ).start()

    for peer in range(n - 1):

        @pl.when(me > peer)
        def _():
            pl.semaphore_signal(
                ready_sem.at[me - 1], inc=1, device_id={"block": peer}, device_id_type=MESH_ID
            )
            send(peer, early)
            if peer == 0:
                send(peer, late)

    plain = [
        (pw_in, pw_b, 0), (pg_in, vec_b.at[0], 1), (ow_in, vec_b.at[1], 1),
        (q_in.at[0], q_b, 2), (qg_in, gain_b.at[0], 3), (kg_in, gain_b.at[1], 3),
    ]
    for src, dst, kind in plain:
        pltpu.make_async_copy(src, dst, local_sem.at[kind]).start()
    for src, buf, part, kind in early + late:
        pltpu.make_async_copy(src, mine(buf, part), recv_sem.at[kind]).start()

    def whole(ref, sem):
        pltpu.make_async_copy(ref, ref, sem).wait()

    whole(pw_b, local_sem.at[0])
    whole(vec_b, local_sem.at[1])
    whole(q_b, local_sem.at[2])
    whole(gain_b, local_sem.at[3])
    kinds = [int_b, cnt_b, kv_b, dkv_b]

    def arrive(kind):
        whole(kinds[kind], recv_sem.at[kind])

    w_s[...] = jnp.zeros_like(w_s)
    w_s[0:FEATS, :] = pw_b[...]
    w = w_s[...]
    centred = w - jnp.mean(w, axis=1, keepdims=True)
    ow = vec_b[1]
    twice = jnp.concatenate([centred, centred], 0)
    gram = dot(
        jnp.concatenate([centred, jnp.broadcast_to(ow * WIDTH, (16, WIDTH))], 0),
        twice, 1, 1, lax.Precision.HIGHEST,
    ) * (1.0 / WIDTH)
    g_hi, g_lo = split(gram)
    gram_s[...] = jnp.concatenate([g_hi, g_lo[:, 0:ROWS]], 1)
    for ref, values in ((wg_s, centred * (vec_b[0] * (1.0 / math.sqrt(DEC_HEAD)))), (wx_s, centred * 2.0)):
        ref[...] = values.astype(BF16)
    o_hi, o_lo = split(ow - jnp.mean(ow, axis=1, keepdims=True))
    line = lax.broadcasted_iota(jnp.int32, (16, WIDTH), 0)
    mid = jnp.where(line == 0, o_hi.astype(F32), jnp.where(line == 1, o_lo.astype(F32), 0.0))
    mid_s[...] = jnp.where(line == 2, 1.0 / WIDTH, mid).astype(BF16)

    rho = lax.broadcasted_iota(jnp.int32, (ROWS, QB), 0)
    lane = lax.broadcasted_iota(jnp.int32, (ROWS, QB), 1)
    which = jnp.where(rho < 3 + 3 * NFREQ, rho - 3, rho - 3 - 3 * NFREQ)
    dim = jnp.where(rho < 3, rho, which >> 3)
    mult = jnp.where(rho < 3, 1, jnp.left_shift(1, which & 7))
    offset = jnp.where(dim == 0, lane >> 6, jnp.where(dim == 1, (lane >> 3) & 7, lane & 7))
    base = (2 * offset + 1 - RES) * mult + jnp.where(rho >= 3 + 3 * NFREQ, RES // 2, 0)
    near_s[...] = jnp.where(rho < 3, base.astype(F32) * (1.0 / RES), jnp.where(rho < FEATS, sine(base), 0.0))
    far_s[...] = jnp.where(rho < 3, 1.0, jnp.where(rho < FEATS, sine(base + RES // 2), 0.0))

    per = q_b.shape[0]
    tokens = n * per
    qf_s[...] = jnp.zeros_like(qf_s)
    for h in range(FLOW_HEAD_COUNT):
        cols = slice(h * FLOW_HEAD_SIZE, (h + 1) * FLOW_HEAD_SIZE)
        x = q_b[:, cols].astype(F32)
        x = x * lax.rsqrt(jnp.mean(x * x, axis=-1, keepdims=True) + 1e-06) * (gain_b[0] * gain_b[1])
        qf_s[h * per : (h + 1) * per, cols] = x
    half = FLOW_HEAD_COUNT * per
    q_s[:, 0:half] = qf_s[...].T.astype(BF16)
    pick_r = lax.broadcasted_iota(jnp.int32, (q_s.shape[0], half), 0)
    pick_c = lax.broadcasted_iota(jnp.int32, (q_s.shape[0], half), 1)
    q_s[:, half:] = jnp.where(pick_c // per == pick_r // FLOW_HEAD_SIZE, 1.0, 0.0).astype(BF16)

    for peer in range(1, n - 1):

        @pl.when(me > peer)
        def _():
            send(peer, late)

    for peer in range(1, n):

        @pl.when(me < peer)
        def _():
            pl.semaphore_wait(ready_sem.at[peer - 1], 1)
            send(peer, early)

    @pl.when(me == 0)
    def _():
        for peer in range(1, n):
            send(peer, late)
        whole(dkv_b.at[0 : n - 1], recv_sem.at[3])

    @pl.when(me > 0)
    def _():
        whole(dkv_b.at[0], recv_sem.at[4])

    for peer in range(2, n):

        @pl.when((me > 0) & (me < peer))
        def _():
            send(peer, late)

    @pl.when(me > 0)
    def _():
        whole(dkv_b.at[0 : n - 2], recv_sem.at[3])

    shift = jnp.where(2 * me < n, 0, 1)
    final = (n - 1) * (1 - shift)

    def place(row, source):
        for part in range(2):
            x = dkv_b[source, part].astype(F32)
            for c in range(WIDTH // 128):
                for twin in range(2):
                    tok_s[part * (WIDTH // 128) + c, pl.ds(2 * per * row + twin, per, stride=2), :] = x[
                        :, c * 128 : (c + 1) * 128
                    ]

    for row in range(n - 1):
        place(row, row + shift)
    arrive(0)
    arrive(1)
    whole(dkv_b.at[0], recv_sem.at[5])
    place(n - 1, final)
    rows_g = GROUP * tokens
    head_r = lax.broadcasted_iota(jnp.int32, (2, 2 * per, GW), 0) * 2
    head_r += lax.broadcasted_iota(jnp.int32, (2, 2 * per, GW), 1) & 1
    own_head = head_r == lax.broadcasted_iota(jnp.int32, (2, 2 * per, GW), 2) // DEC_HEAD

    def blocks(first):
        x = jnp.concatenate([tok_s[first // 128 + i] for i in range(GW // 128)], 1)
        x = x.reshape(n, 1, 2 * per, GW)
        return jnp.where(own_head[None], x, 0.0).reshape(rows_g, GW).astype(BF16)

    def left_of(b):
        b_hi, b_lo = split(b)
        return jnp.concatenate([b_hi, b_hi, b_lo], 1)

    left, right = [], []
    for g in range(GROUPS):
        cols = slice(g * GW, (g + 1) * GW)
        left.append(left_of(dot(blocks(g * GW), wg_s[:, cols], 1, 1)))
        vb = blocks(WIDTH + g * GW)
        right.append(left_of(dot(vb, wx_s[:, cols], 1, 1)))
        y = dot(jnp.concatenate([vb, mid_s[:, cols]], 0), vb, 1, 1)
        y_hi = y.astype(BF16).astype(F32)
        y_lo = y - y_hi
        form_s[g] = jnp.concatenate([y_hi[0:rows_g], y_lo[0:rows_g], y_hi[rows_g : rows_g + 8], y_lo[rows_g : rows_g + 8]], 0).astype(BF16)

    slot = lax.broadcasted_iota(jnp.int32, (1, CAP), 1)
    number = jnp.zeros((1, CAP), F32)
    for s in range(n):
        hit = (int_b[s, 1] == me) & (slot < cnt_b[s])
        number += jnp.where(hit, (int_b[s, 0] + 1).astype(F32), 0.0)
    number = jnp.sum(number, axis=1, keepdims=True)
    present = number > 0.5
    block = jnp.maximum(number - 1.0, 0.0).astype(jnp.int32)
    rows1 = lax.broadcasted_iota(jnp.int32, (ROWS, 128), 0)
    which1 = jnp.where(rows1 < 3 + 3 * NFREQ, rows1 - 3, rows1 - 3 - 3 * NFREQ)
    dim1 = jnp.where(rows1 < 3, rows1, which1 >> 3)
    mult1 = jnp.where(rows1 < 3, 1, jnp.left_shift(1, which1 & 7))
    cell = jnp.where(
        dim1 == 0, block >> 12, jnp.where(dim1 == 1, (block >> 6) & (PER_SIDE - 1), block & (PER_SIDE - 1))
    )
    cell = cell * mult1 * (2 * SIDE)
    turn = jnp.where(rows1 < 3, 1.0, sine(cell + RES // 2))
    step = jnp.where(rows1 < 3, cell.astype(F32) * (1.0 / RES), sine(cell))
    feats = near_s[...] * jnp.concatenate([turn] * (QB // 128), 1)
    feats += far_s[...] * jnp.concatenate([step] * (QB // 128), 1)
    f_hi, f_lo = split(feats)
    f3 = jnp.concatenate([f_hi, f_lo, f_hi], 0)

    scores = dot(jnp.concatenate(left + [gram_s[...]] + right, 0), f3, 1, 0)
    below = GROUPS * rows_g
    spread = jnp.sum(scores[below : below + ROWS] * feats, axis=0, keepdims=True)
    logit = scores[below + ROWS : below + ROWS + 1]
    rstd = lax.rsqrt(spread + 1e-05)

    squares = jnp.zeros((8, QB), F32)
    linear = jnp.zeros((8, QB), F32)
    for g in range(GROUPS):
        score = scores[g * rows_g : (g + 1) * rows_g] * rstd
        score = score.reshape(n, 2, 2 * per, QB)
        top = jnp.max(score, axis=0)
        top = jnp.maximum(top, pltpu.roll(top, 4, 1))
        top = jnp.maximum(top, pltpu.roll(top, 2, 1))
        e = jnp.exp(score - top[None])
        total = jnp.sum(e, axis=0)
        total = total + pltpu.roll(total, 4, 1)
        total = total + pltpu.roll(total, 2, 1)
        probs = (e * (1.0 / total)[None]).reshape(rows_g, QB).astype(BF16)
        out = dot(form_s[g], probs, 1, 0)
        cross = scores[below + ROWS + 16 + g * rows_g : below + ROWS + 16 + (g + 1) * rows_g]
        cross += out[0:rows_g] + out[rows_g : 2 * rows_g]
        squares += jnp.sum((cross * probs.astype(F32)).reshape(-1, 8, QB), axis=0)
        linear += out[2 * rows_g : 2 * rows_g + 8] + out[2 * rows_g + 8 :]
    mean = linear[2:3]
    logit += linear[0:1] + linear[1:2]
    var = spread + jnp.sum(squares, axis=0, keepdims=True) * (1.0 / WIDTH) - mean * mean
    occ = logit * lax.rsqrt(jnp.maximum(var, 0.0) + 1e-05)
    occ_out[0] = jnp.where(present, occ, 0.0)

    arrive(2)
    for s in range(n):
        kf_s[s * per : (s + 1) * per, :] = kv_b[s, 0].astype(F32)
        vf_s[s * per : (s + 1) * per, :] = kv_b[s, 1].astype(F32)
    keys = kf_s[...]
    s_hi, s_lo = split(keys * keys)
    both = dot(jnp.concatenate([keys.astype(BF16), s_hi, s_lo], 0), q_s[...], 1, 0)
    size = pltpu.roll(both[tokens : 2 * tokens] + both[2 * tokens :], half, 1)
    size = lax.rsqrt(size * (1.0 / FLOW_HEAD_SIZE) + 1e-06) * (1.0 / math.sqrt(FLOW_HEAD_SIZE))
    score = both[0:tokens] * size
    weights = jnp.exp(score - jnp.max(score, axis=0, keepdims=True))
    inverse = jnp.broadcast_to(1.0 / jnp.sum(weights, axis=0, keepdims=True), (8, 2 * half))
    turned = jnp.concatenate([weights, inverse], 0).T
    for r in range(FLOW_HEAD_COUNT // 2):
        cols = slice(2 * r * FLOW_HEAD_SIZE, 2 * (r + 1) * FLOW_HEAD_SIZE)
        rows = turned[2 * r * per : 2 * (r + 1) * per]
        mixed = dot(rows[:, 0:tokens].astype(BF16), vf_s[:, cols].astype(BF16), 1, 0)
        mixed = mixed * rows[:, tokens : tokens + 1]
        mixed = jnp.concatenate([mixed[0:per, 0:FLOW_HEAD_SIZE], mixed[per:, FLOW_HEAD_SIZE:]], 1)
        flow_out[0, :, cols] = mixed.astype(BF16)

    for kind, buf in enumerate(kinds):
        whole(buf.at[0 : n - 1], send_sem.at[kind])


def write_out(flow_ref, occ_ref, flow_out, occ_out, sem):
    copies = [
        pltpu.make_async_copy(flow_ref, flow_out, sem.at[0]),
        pltpu.make_async_copy(occ_ref, occ_out, sem.at[1]),
    ]
    for copy in copies:
        copy.start()
    for copy in copies:
        copy.wait()


def fused_body(*args):
    (q, k, v, qg, kg, dk, dv, ids, counts, pages, pw, pg, ow) = args
    n = lax.axis_size("block")
    per = q.shape[1]
    tokens = n * per
    flow_width = q.shape[2]
    qg, kg, pg, ow = (x.reshape(1, -1) for x in (qg, kg, pg, ow))
    vmem = pltpu.VMEM
    made = pl.pallas_call(
        lambda *refs: fused_kernel(n, *refs),
        out_shape=(pltpu.VMEM(q.shape, BF16), pltpu.VMEM((1, PAGES, QB), F32)),
        in_specs=[pl.BlockSpec(memory_space=pltpu.HBM)] * 13,
        out_specs=(pl.BlockSpec(memory_space=pltpu.VMEM), pl.BlockSpec(memory_space=pltpu.VMEM)),
        scratch_shapes=[
            vmem((per, flow_width), BF16),
            vmem((n, 2, per, flow_width), BF16),
            vmem((n, 2, per, WIDTH), BF16),
            vmem((n, 2, 1, CAP), jnp.int32),
            vmem((n, 1, 1), jnp.int32),
            vmem((2, 1, FLOW_HEAD_SIZE), F32),
            vmem((2, 1, WIDTH), F32),
            vmem((FEATS, WIDTH), F32),
            vmem((ROWS, WIDTH), F32),
            vmem((ROWS, WIDTH), BF16),
            vmem((ROWS, WIDTH), BF16),
            vmem((ROWS + 16, 3 * ROWS), BF16),
            vmem((16, WIDTH), BF16),
            vmem((ROWS, QB), F32),
            vmem((ROWS, QB), F32),
            vmem((FLOW_HEAD_COUNT * per, flow_width), F32),
            vmem((flow_width, 2 * FLOW_HEAD_COUNT * per), BF16),
            vmem((GROUPS, 2 * GROUP * tokens + 16, ROWS), BF16),
            vmem((2 * WIDTH // 128, 2 * tokens, 128), F32),
            vmem((tokens, flow_width), F32),
            vmem((tokens, flow_width), F32),
            pltpu.SemaphoreType.DMA((4,)),
            pltpu.SemaphoreType.DMA((6,)),
            pltpu.SemaphoreType.DMA((4,)),
            pltpu.SemaphoreType.REGULAR((n - 1,)),
        ],
        compiler_params=pltpu.CompilerParams(collective_id=0, has_side_effects=True),
    )(q, k, v, qg, kg, dk, dv, ids, counts, pages, pw, pg, ow)
    made = tuple(pltpu.with_memory_space_constraint(x, pltpu.VMEM) for x in made)
    return pl.pallas_call(
        write_out,
        out_shape=tuple(jax.ShapeDtypeStruct(x.shape, x.dtype) for x in made),
        in_specs=[pl.BlockSpec(memory_space=pltpu.VMEM)] * 2,
        out_specs=(pl.BlockSpec(memory_space=pltpu.HBM),) * 2,
        scratch_shapes=[pltpu.SemaphoreType.DMA((2,))],
    )(*made)


def solution(mesh):
    return jax.shard_map(
        fused_body if mesh.shape["block"] * 4 == 4 * GROUP else body,
        mesh=mesh,
        in_specs=(
            P(("groups", "shape"), "block", None),
            P(("groups", "shape"), "block", None),
            P(("groups", "shape"), "block", None),
            P(),
            P(),
            P(("groups", "shape"), "block", None),
            P(("groups", "shape"), "block", None),
            P(("groups", "shape"), "block"),
            P(("groups", "shape"), "block"),
            P(("groups", "shape"), "block"),
            P(),
            P(),
            P(),
        ),
        out_specs=(P(("groups", "shape"), "block", None), P(("groups", "shape"), "block", None)),
        check_vma=False,
    )
```

```python
import math

import jax
import jax.numpy as jnp
from jax import lax
from jax.experimental import pallas as pl
from jax.experimental.pallas import tpu as pltpu
from jax.sharding import PartitionSpec as P

FLOW_HEAD_COUNT = 16
FLOW_HEAD_SIZE = 128
DEC_HEADS = 16
DEC_HEAD = 64
NFREQ = 8
RES = 512
SIDE = 8
PAGES = 1
QB = 512
PER_SIDE = 64


def norm_per_head(values_in, gain, head_count):
    flat_rows = values_in.shape[0]
    entries = values_in.astype(jnp.float32).reshape(flat_rows, head_count, -1)
    scaled = entries * lax.rsqrt(jnp.mean(entries * entries, axis=-1, keepdims=True) + 1e-06)
    return (scaled * gain).reshape(flat_rows, -1).astype(jnp.bfloat16)


def query_points(block_id):
    point_index = jnp.arange(QB, dtype=jnp.int32)
    cell_index = [
        block_id // (PER_SIDE * PER_SIDE) * SIDE + point_index // (SIDE * SIDE),
        block_id // PER_SIDE % PER_SIDE * SIDE + point_index // SIDE % SIDE,
        block_id % PER_SIDE * SIDE + point_index % SIDE,
    ]
    coords = jnp.stack(
        [(cell.astype(jnp.float32) + 0.5) * (2.0 / RES) - 1.0 for cell in cell_index], 0
    )
    frequency = math.pi * 2.0 ** jnp.arange(NFREQ).astype(jnp.float32)
    phases = (coords[:, None, :] * frequency[None, :, None]).reshape(3 * NFREQ, QB)
    return jnp.concatenate([coords, jnp.sin(phases), jnp.cos(phases)], 0)


def decode_block(block_id, k_heads, v_heads, point_weight, point_gain, occupancy_weight):
    features = query_points(block_id)
    start_proj = lax.dot_general(
        features,
        point_weight,
        (((0,), (0,)), ((), ())),
        precision=lax.Precision.HIGHEST,
        preferred_element_type=jnp.float32,
    )
    row_mean = jnp.mean(start_proj, axis=-1, keepdims=True)
    centred = start_proj - row_mean
    row_var = jnp.mean(centred * centred, axis=-1, keepdims=True)
    point_query = (centred * lax.rsqrt(row_var + 1e-05) * point_gain).astype(jnp.bfloat16)
    q_heads = jnp.transpose(point_query.reshape(QB, DEC_HEADS, DEC_HEAD), (1, 0, 2))

    def one_head(head_item):
        q_head, k_head, v_head = head_item
        score_matrix = jnp.dot(q_head, k_head.T, preferred_element_type=jnp.float32) / math.sqrt(
            DEC_HEAD
        )
        row_maximum = jnp.max(score_matrix, axis=-1, keepdims=True)
        weights = jnp.exp(score_matrix - row_maximum)
        row_sum = jnp.sum(weights, axis=-1, keepdims=True)
        mixed = jnp.dot(weights.astype(jnp.bfloat16), v_head, preferred_element_type=jnp.float32)
        return mixed / row_sum

    per_head = lax.map(one_head, (q_heads, k_heads, v_heads))
    hidden = start_proj + jnp.transpose(per_head, (1, 0, 2)).reshape(QB, -1)
    hid_mean = jnp.mean(hidden, axis=-1, keepdims=True)
    hid_centred = hidden - hid_mean
    hid_var = jnp.mean(hid_centred * hid_centred, axis=-1, keepdims=True)
    normed = hid_centred * lax.rsqrt(hid_var + 1e-05)
    return jnp.dot(
        normed,
        occupancy_weight,
        precision=lax.Precision.HIGHEST,
        preferred_element_type=jnp.float32,
    )


def decode_many(id_list, owner_list, k_all, value_all, point_weight, point_gain, occupancy_weight):

    def one_block(block_item):
        block_id, owner_shape = block_item
        k_heads = lax.dynamic_index_in_dim(k_all, owner_shape, 0, keepdims=False)
        v_heads = lax.dynamic_index_in_dim(value_all, owner_shape, 0, keepdims=False)
        return decode_block(block_id, k_heads, v_heads, point_weight, point_gain, occupancy_weight)

    return lax.map(one_block, (id_list, owner_list))


def body(
    query,
    raw_flow_keys,
    flow_value_input,
    query_norm_gain,
    key_norm_gain,
    dec_keys,
    dec_values,
    block_ids,
    counts,
    page_of,
    point_weight,
    point_gain,
    occupancy_weight,
):
    shape_number, token_rows, feature_width = query.shape
    scale_per_head = 1.0 / math.sqrt(FLOW_HEAD_SIZE)
    normed_queries = norm_per_head(
        query.reshape(shape_number * token_rows, feature_width), query_norm_gain, FLOW_HEAD_COUNT
    )
    normed_queries = normed_queries.reshape(shape_number, token_rows, feature_width)
    normed_keys = norm_per_head(
        raw_flow_keys.reshape(shape_number * token_rows, feature_width),
        key_norm_gain,
        FLOW_HEAD_COUNT,
    )
    normed_keys = normed_keys.reshape(shape_number, token_rows, feature_width)
    latents = (
        lax.all_gather(dec_keys, "block", axis=1, tiled=True),
        lax.all_gather(dec_values, "block", axis=1, tiled=True),
    )
    peer_total = lax.axis_size("block")
    query_split = normed_queries.reshape(shape_number, token_rows, FLOW_HEAD_COUNT, FLOW_HEAD_SIZE)
    row_maximum = jnp.full((shape_number, FLOW_HEAD_COUNT, token_rows), -1e30, jnp.float32)
    k_piece = lax.all_gather(normed_keys, "block", axis=1, tiled=True).reshape(
        shape_number, -1, FLOW_HEAD_COUNT, FLOW_HEAD_SIZE
    )
    v_piece = lax.all_gather(flow_value_input, "block", axis=1, tiled=True).reshape(
        shape_number, -1, FLOW_HEAD_COUNT, FLOW_HEAD_SIZE
    )
    score_matrix = (
        jnp.einsum("sqhe,skhe->shqk", query_split, k_piece, preferred_element_type=jnp.float32)
        * scale_per_head
    )
    new_max = jnp.maximum(row_maximum, jnp.max(score_matrix, axis=-1))
    weights = jnp.exp(score_matrix - new_max[..., None])
    row_sum = jnp.sum(weights, axis=-1)
    mixed_sum = jnp.einsum(
        "shqk,skhe->shqe", weights.astype(jnp.bfloat16), v_piece, preferred_element_type=jnp.float32
    )
    row_maximum, row_sum, mixed_sum = (new_max, row_sum, mixed_sum)
    attended = mixed_sum / row_sum[..., None]
    flow_out = (
        jnp.transpose(attended, (0, 2, 1, 3))
        .reshape(shape_number, token_rows, feature_width)
        .astype(jnp.bfloat16)
    )
    key_rows, value_rows = latents
    k_all = jnp.transpose(key_rows.reshape(shape_number, -1, DEC_HEADS, DEC_HEAD), (0, 2, 1, 3))
    value_all = jnp.transpose(
        value_rows.reshape(shape_number, -1, DEC_HEADS, DEC_HEAD), (0, 2, 1, 3)
    )
    slot_count = block_ids.shape[1]
    slot_index = jnp.arange(slot_count, dtype=jnp.int32)
    live_mask = slot_index[None, :] < counts
    dest_peer = page_of // PAGES
    local_page = page_of % PAGES
    peer_ids = jnp.arange(peer_total, dtype=jnp.int32)
    route = (dest_peer[:, None, :] == peer_ids[None, :, None]) & live_mask[:, None, :]
    page_tag = jnp.where(
        jnp.any(route, axis=-1), jnp.sum(jnp.where(route, local_page[:, None, :], 0), axis=-1), -1
    )
    page_tag = jnp.transpose(page_tag)
    page_range = jnp.arange(PAGES, dtype=jnp.int32)
    send_ids = jnp.transpose(jnp.sum(jnp.where(route, block_ids[:, None, :], 0), axis=-1))
    recv_ids, recv_tag = (
        lax.all_to_all(send_ids, "block", split_axis=0, concat_axis=0, tiled=True),
        lax.all_to_all(page_tag, "block", split_axis=0, concat_axis=0, tiled=True),
    )
    page_match = recv_tag[None, :, :] == page_range[:, None, None]
    chosen = jnp.sum(jnp.where(page_match, recv_ids[None, :, :], 0), axis=1)
    present = jnp.transpose(jnp.any(page_match, axis=1))
    owner_list = jnp.repeat(jnp.arange(shape_number, dtype=jnp.int32), PAGES)
    occ_rows = decode_many(
        jnp.transpose(chosen).reshape(-1),
        owner_list,
        k_all,
        value_all,
        point_weight,
        point_gain,
        occupancy_weight,
    )
    occ_rows = occ_rows.reshape(shape_number, PAGES, QB)
    occupancy = jnp.where(present[:, :, None], occ_rows, jnp.zeros_like(occ_rows))
    return (flow_out, occupancy)


F32, BF16 = jnp.float32, jnp.bfloat16
MESH_ID = pl.DeviceIdType.MESH
WIDTH = DEC_HEADS * DEC_HEAD
FEATS = 3 + 6 * NFREQ
ROWS = 64
GROUP = 4
GROUPS = DEC_HEADS // GROUP
GW = GROUP * DEC_HEAD
CAP = 4


def split(x):
    hi = x.astype(BF16)
    return hi, (x - hi.astype(F32)).astype(BF16)


def dot(a, b, ca, cb, precision=None):
    return lax.dot_general(
        a, b, (((ca,), (cb,)), ((), ())), precision=precision, preferred_element_type=F32
    )


def sine(r):
    r = ((r + 512) & 1023) - 512
    r = jnp.where(r > 256, 512 - r, jnp.where(r < -256, -512 - r, r))
    x = r.astype(F32) * (math.pi / 512)
    x2 = x * x
    acc = jnp.full_like(x, 1.0 / math.factorial(13))
    for order in (11, 9, 7, 5, 3, 1):
        sign = 1.0 if order % 4 == 1 else -1.0
        acc = acc * x2 + sign / math.factorial(order)
    return acc * x


def fused_kernel(
    n, q_in, k_in, v_in, qg_in, kg_in, dk_in, dv_in, id_in, cnt_in, page_in, pw_in, pg_in, ow_in,
    flow_out, occ_out,
    q_b, kv_b, dkv_b, int_b, cnt_b, gain_b, vec_b, pw_b,
    w_s, wg_s, wx_s, gram_s, mid_s, near_s, far_s, qf_s, q_s, form_s, tok_s, rows_s, kf_s, vf_s,
    send_sem, recv_sem, local_sem, ready_sem,
):
    me = lax.axis_index("block")
    barrier = pltpu.get_barrier_semaphore()
    for peer in range(1, n):

        @pl.when(me < peer)
        def _():
            pl.semaphore_signal(barrier, inc=1, device_id={"block": peer}, device_id_type=MESH_ID)

    @pl.when(me > 0)
    def _():
        pl.semaphore_wait(barrier, me)

    early = [
        (id_in, int_b, 0, 0), (page_in, int_b, 1, 0), (cnt_in, cnt_b, None, 1),
        (dk_in.at[0], dkv_b, 0, 3), (dv_in.at[0], dkv_b, 1, 3),
    ]
    late = [(k_in.at[0], kv_b, 0, 2), (v_in.at[0], kv_b, 1, 2)]

    def mine(buf, part):
        return buf.at[me] if part is None else buf.at[me, part]

    def send(peer, moved):
        final = n - 1 if 2 * peer < n else 0
        for src, buf, part, kind in moved:
            into = kind
            out = 4 if peer == 0 and kind == 2 else kind
            if kind == 3:
                into = jnp.where(me == final, 5, jnp.where(me == peer - 1, 4, 3))
            pltpu.make_async_remote_copy(
                src_ref=src, dst_ref=mine(buf, part),
                send_sem=send_sem.at[out], recv_sem=recv_sem.at[into],
                device_id={"block": peer}, device_id_type=MESH_ID,
            ).start()

    for peer in range(n - 1):

        @pl.when(me > peer)
        def _():
            pl.semaphore_signal(
                ready_sem.at[me - 1], inc=1, device_id={"block": peer}, device_id_type=MESH_ID
            )
            send(peer, early)
            if peer == 0:
                send(peer, late)

    plain = [
        (pw_in, pw_b, 0), (pg_in, vec_b.at[0], 1), (ow_in, vec_b.at[1], 1),
        (q_in.at[0], q_b, 2), (qg_in, gain_b.at[0], 3), (kg_in, gain_b.at[1], 3),
    ]
    for src, dst, kind in plain:
        pltpu.make_async_copy(src, dst, local_sem.at[kind]).start()
    for src, buf, part, kind in early + late:
        pltpu.make_async_copy(src, mine(buf, part), recv_sem.at[kind]).start()

    def whole(ref, sem):
        pltpu.make_async_copy(ref, ref, sem).wait()

    whole(pw_b, local_sem.at[0])
    whole(vec_b, local_sem.at[1])
    whole(q_b, local_sem.at[2])
    whole(gain_b, local_sem.at[3])
    kinds = [int_b, cnt_b, kv_b, dkv_b]

    def arrive(kind):
        whole(kinds[kind], recv_sem.at[kind])

    w_s[...] = jnp.zeros_like(w_s)
    w_s[0:FEATS, :] = pw_b[...]
    w = w_s[...]
    centred = w - jnp.mean(w, axis=1, keepdims=True)
    ow = vec_b[1]
    twice = jnp.concatenate([centred, centred], 0)
    gram = dot(
        jnp.concatenate([centred, jnp.broadcast_to(ow * WIDTH, (16, WIDTH))], 0),
        twice, 1, 1, lax.Precision.HIGHEST,
    ) * (1.0 / WIDTH)
    g_hi, g_lo = split(gram)
    gram_s[...] = jnp.concatenate([g_hi, g_lo[:, 0:ROWS]], 1)
    for ref, values in ((wg_s, centred * (vec_b[0] * (1.0 / math.sqrt(DEC_HEAD)))), (wx_s, centred * 2.0)):
        ref[...] = values.astype(BF16)
    o_hi, o_lo = split(ow - jnp.mean(ow, axis=1, keepdims=True))
    line = lax.broadcasted_iota(jnp.int32, (16, WIDTH), 0)
    mid = jnp.where(line == 0, o_hi.astype(F32), jnp.where(line == 1, o_lo.astype(F32), 0.0))
    mid_s[...] = jnp.where(line == 2, 1.0 / WIDTH, mid).astype(BF16)

    rho = lax.broadcasted_iota(jnp.int32, (ROWS, QB), 0)
    lane = lax.broadcasted_iota(jnp.int32, (ROWS, QB), 1)
    which = jnp.where(rho < 3 + 3 * NFREQ, rho - 3, rho - 3 - 3 * NFREQ)
    dim = jnp.where(rho < 3, rho, which >> 3)
    mult = jnp.where(rho < 3, 1, jnp.left_shift(1, which & 7))
    offset = jnp.where(dim == 0, lane >> 6, jnp.where(dim == 1, (lane >> 3) & 7, lane & 7))
    base = (2 * offset + 1 - RES) * mult + jnp.where(rho >= 3 + 3 * NFREQ, RES // 2, 0)
    near_s[...] = jnp.where(rho < 3, base.astype(F32) * (1.0 / RES), jnp.where(rho < FEATS, sine(base), 0.0))
    far_s[...] = jnp.where(rho < 3, 1.0, jnp.where(rho < FEATS, sine(base + RES // 2), 0.0))

    per = q_b.shape[0]
    tokens = n * per
    pair = 2 * FLOW_HEAD_SIZE
    pick_r = lax.broadcasted_iota(jnp.int32, qf_s.shape, 0)
    pick_c = lax.broadcasted_iota(jnp.int32, qf_s.shape, 1)
    qf_s[...] = jnp.where((pick_r // per) % 4 == 2 + pick_c // FLOW_HEAD_SIZE, 1.0, 0.0)
    for h in range(FLOW_HEAD_COUNT):
        cols = slice(h * FLOW_HEAD_SIZE, (h + 1) * FLOW_HEAD_SIZE)
        x = q_b[:, cols].astype(F32)
        x = x * lax.rsqrt(jnp.mean(x * x, axis=-1, keepdims=True) + 1e-06) * (gain_b[0] * gain_b[1])
        row = (h // 2) * 4 * per + (h % 2) * per
        qf_s[row : row + per, (h % 2) * FLOW_HEAD_SIZE : (h % 2 + 1) * FLOW_HEAD_SIZE] = x
    q_s[...] = qf_s[...].astype(BF16)

    @pl.when(me > 0)
    def _():
        whole(kv_b.at[0], send_sem.at[4])

    for peer in range(1, n - 1):

        @pl.when(me > peer)
        def _():
            send(peer, late)

    for peer in range(1, n):

        @pl.when(me < peer)
        def _():
            pl.semaphore_wait(ready_sem.at[peer - 1], 1)
            send(peer, early)

    @pl.when(me == 0)
    def _():
        for peer in range(1, n):
            send(peer, late)
        whole(dkv_b.at[0 : n - 1], recv_sem.at[3])

    @pl.when(me > 0)
    def _():
        whole(dkv_b.at[0], recv_sem.at[4])

    for peer in range(2, n):

        @pl.when((me > 0) & (me < peer))
        def _():
            send(peer, late)

    @pl.when(me > 0)
    def _():
        whole(dkv_b.at[0 : n - 2], recv_sem.at[3])

    shift = jnp.where(2 * me < n, 0, 1)
    final = (n - 1) * (1 - shift)

    rows_g = GROUP * tokens
    span = 4 * per
    head_r = lax.broadcasted_iota(jnp.int32, (2, 2 * per, GW), 0) * 2
    head_r += lax.broadcasted_iota(jnp.int32, (2, 2 * per, GW), 1) & 1
    own_head = head_r == lax.broadcasted_iota(jnp.int32, (2, 2 * per, GW), 2) // DEC_HEAD
    tiles = WIDTH // 128

    def place(row, source):
        for part in range(2):
            x = dkv_b[source, part].astype(F32)
            for c in range(tiles):
                for twin in range(2):
                    tok_s[part * tiles + c, pl.ds(2 * per * row + twin, per, stride=2), :] = x[
                        :, c * 128 : (c + 1) * 128
                    ]
            for g in range(GROUPS):
                first = part * tiles + g * GW // 128
                y = jnp.concatenate(
                    [tok_s[first + i, 2 * per * row : 2 * per * (row + 1), :] for i in range(GW // 128)], 1
                )
                y = jnp.where(own_head, y[None], 0.0).reshape(span, GW).astype(BF16)
                rows_s[part * GROUPS + g, row * span : (row + 1) * span, :] = y

    for row in range(n - 1):
        place(row, row + shift)
    arrive(0)
    arrive(1)
    whole(dkv_b.at[0], recv_sem.at[5])
    place(n - 1, final)

    def left_of(b):
        b_hi, b_lo = split(b)
        return jnp.concatenate([b_hi, b_hi, b_lo], 1)

    left, right = [], []
    for g in range(GROUPS):
        cols = slice(g * GW, (g + 1) * GW)
        left.append(left_of(dot(rows_s[g], wg_s[:, cols], 1, 1)))
        vb = rows_s[GROUPS + g]
        right.append(left_of(dot(vb, wx_s[:, cols], 1, 1)))
        y = dot(jnp.concatenate([vb, mid_s[:, cols]], 0), vb, 1, 1)
        y_hi = y.astype(BF16).astype(F32)
        y_lo = y - y_hi
        form_s[g] = jnp.concatenate([y_hi[0:rows_g], y_lo[0:rows_g], y_hi[rows_g : rows_g + 8], y_lo[rows_g : rows_g + 8]], 0).astype(BF16)

    slot = lax.broadcasted_iota(jnp.int32, (1, CAP), 1)
    number = jnp.zeros((1, CAP), F32)
    for s in range(n):
        hit = (int_b[s, 1] == me) & (slot < cnt_b[s])
        number += jnp.where(hit, (int_b[s, 0] + 1).astype(F32), 0.0)
    number = jnp.sum(number, axis=1, keepdims=True)
    present = number > 0.5
    block = jnp.maximum(number - 1.0, 0.0).astype(jnp.int32)
    rows1 = lax.broadcasted_iota(jnp.int32, (ROWS, 128), 0)
    which1 = jnp.where(rows1 < 3 + 3 * NFREQ, rows1 - 3, rows1 - 3 - 3 * NFREQ)
    dim1 = jnp.where(rows1 < 3, rows1, which1 >> 3)
    mult1 = jnp.where(rows1 < 3, 1, jnp.left_shift(1, which1 & 7))
    cell = jnp.where(
        dim1 == 0, block >> 12, jnp.where(dim1 == 1, (block >> 6) & (PER_SIDE - 1), block & (PER_SIDE - 1))
    )
    cell = cell * mult1 * (2 * SIDE)
    turn = jnp.where(rows1 < 3, 1.0, sine(cell + RES // 2))
    step = jnp.where(rows1 < 3, cell.astype(F32) * (1.0 / RES), sine(cell))
    feats = near_s[...] * jnp.concatenate([turn] * (QB // 128), 1)
    feats += far_s[...] * jnp.concatenate([step] * (QB // 128), 1)
    f_hi, f_lo = split(feats)
    f3 = jnp.concatenate([f_hi, f_lo, f_hi], 0)

    scores = dot(jnp.concatenate(left + [gram_s[...]] + right, 0), f3, 1, 0)
    below = GROUPS * rows_g
    spread = jnp.sum(scores[below : below + ROWS] * feats, axis=0, keepdims=True)
    logit = scores[below + ROWS : below + ROWS + 1]
    rstd = lax.rsqrt(spread + 1e-05)

    squares = jnp.zeros((8, QB), F32)
    linear = jnp.zeros((8, QB), F32)
    for g in range(GROUPS):
        score = scores[g * rows_g : (g + 1) * rows_g] * rstd
        score = score.reshape(n, 2, 2 * per, QB)
        top = jnp.max(score, axis=0)
        top = jnp.maximum(top, pltpu.roll(top, 4, 1))
        top = jnp.maximum(top, pltpu.roll(top, 2, 1))
        e = jnp.exp(score - top[None])
        total = jnp.sum(e, axis=0)
        total = total + pltpu.roll(total, 4, 1)
        total = total + pltpu.roll(total, 2, 1)
        probs = (e * (1.0 / total)[None]).reshape(rows_g, QB).astype(BF16)
        out = dot(form_s[g], probs, 1, 0)
        cross = scores[below + ROWS + 16 + g * rows_g : below + ROWS + 16 + (g + 1) * rows_g]
        cross += out[0:rows_g] + out[rows_g : 2 * rows_g]
        squares += jnp.sum((cross * probs.astype(F32)).reshape(-1, 8, QB), axis=0)
        linear += out[2 * rows_g : 2 * rows_g + 8] + out[2 * rows_g + 8 :]
    mean = linear[2:3]
    logit += linear[0:1] + linear[1:2]
    var = spread + jnp.sum(squares, axis=0, keepdims=True) * (1.0 / WIDTH) - mean * mean
    occ = logit * lax.rsqrt(jnp.maximum(var, 0.0) + 1e-05)
    occ_out[0] = jnp.where(present, occ, 0.0)

    arrive(2)
    for s in range(n):
        kf_s[s * per : (s + 1) * per, :] = kv_b[s, 0].astype(F32)
        vf_s[s * per : (s + 1) * per, :] = kv_b[s, 1].astype(F32)
    score, size = [], []
    for r in range(FLOW_HEAD_COUNT // 2):
        keys = kf_s[:, r * pair : (r + 1) * pair]
        s_hi, s_lo = split(keys * keys)
        rows = q_s[r * 4 * per : (r + 1) * 4 * per, :]
        score.append(dot(rows, keys.astype(BF16), 1, 1)[0 : 2 * per])
        size.append((dot(rows, s_hi, 1, 1) + dot(rows, s_lo, 1, 1))[2 * per :])
    score, size = jnp.concatenate(score, 0), jnp.concatenate(size, 0)
    size = lax.rsqrt(size * (1.0 / FLOW_HEAD_SIZE) + 1e-06) * (1.0 / math.sqrt(FLOW_HEAD_SIZE))
    score = score * size
    weights = jnp.exp(score - jnp.max(score, axis=-1, keepdims=True))
    inverse = 1.0 / jnp.sum(weights, axis=-1, keepdims=True)
    for r in range(FLOW_HEAD_COUNT // 2):
        cols = slice(2 * r * FLOW_HEAD_SIZE, 2 * (r + 1) * FLOW_HEAD_SIZE)
        rows = slice(2 * r * per, 2 * (r + 1) * per)
        mixed = dot(weights[rows].astype(BF16), vf_s[:, cols].astype(BF16), 1, 0) * inverse[rows]
        mixed = jnp.concatenate([mixed[0:per, 0:FLOW_HEAD_SIZE], mixed[per:, FLOW_HEAD_SIZE:]], 1)
        flow_out[0, :, cols] = mixed.astype(BF16)

    for kind, buf in enumerate(kinds):
        if kind != 2:
            whole(buf.at[0 : n - 1], send_sem.at[kind])

    @pl.when(me > 0)
    def _():
        whole(kv_b.at[0 : n - 2], send_sem.at[2])

    @pl.when(me == 0)
    def _():
        whole(kv_b.at[0 : n - 1], send_sem.at[2])


def write_out(flow_ref, occ_ref, flow_out, occ_out, sem):
    copies = [
        pltpu.make_async_copy(flow_ref, flow_out, sem.at[0]),
        pltpu.make_async_copy(occ_ref, occ_out, sem.at[1]),
    ]
    for copy in copies:
        copy.start()
    for copy in copies:
        copy.wait()


def fused_body(*args):
    (q, k, v, qg, kg, dk, dv, ids, counts, pages, pw, pg, ow) = args
    n = lax.axis_size("block")
    per = q.shape[1]
    tokens = n * per
    flow_width = q.shape[2]
    qg, kg, pg, ow = (x.reshape(1, -1) for x in (qg, kg, pg, ow))
    vmem = pltpu.VMEM
    made = pl.pallas_call(
        lambda *refs: fused_kernel(n, *refs),
        out_shape=(pltpu.VMEM(q.shape, BF16), pltpu.VMEM((1, PAGES, QB), F32)),
        in_specs=[pl.BlockSpec(memory_space=pltpu.HBM)] * 13,
        out_specs=(pl.BlockSpec(memory_space=pltpu.VMEM), pl.BlockSpec(memory_space=pltpu.VMEM)),
        scratch_shapes=[
            vmem((per, flow_width), BF16),
            vmem((n, 2, per, flow_width), BF16),
            vmem((n, 2, per, WIDTH), BF16),
            vmem((n, 2, 1, CAP), jnp.int32),
            vmem((n, 1, 1), jnp.int32),
            vmem((2, 1, FLOW_HEAD_SIZE), F32),
            vmem((2, 1, WIDTH), F32),
            vmem((FEATS, WIDTH), F32),
            vmem((ROWS, WIDTH), F32),
            vmem((ROWS, WIDTH), BF16),
            vmem((ROWS, WIDTH), BF16),
            vmem((ROWS + 16, 3 * ROWS), BF16),
            vmem((16, WIDTH), BF16),
            vmem((ROWS, QB), F32),
            vmem((ROWS, QB), F32),
            vmem((2 * FLOW_HEAD_COUNT * per, 2 * FLOW_HEAD_SIZE), F32),
            vmem((2 * FLOW_HEAD_COUNT * per, 2 * FLOW_HEAD_SIZE), BF16),
            vmem((GROUPS, 2 * GROUP * tokens + 16, ROWS), BF16),
            vmem((2 * WIDTH // 128, 2 * tokens, 128), F32),
            vmem((2 * GROUPS, GROUP * tokens, GW), BF16),
            vmem((tokens, flow_width), F32),
            vmem((tokens, flow_width), F32),
            pltpu.SemaphoreType.DMA((5,)),
            pltpu.SemaphoreType.DMA((6,)),
            pltpu.SemaphoreType.DMA((4,)),
            pltpu.SemaphoreType.REGULAR((n - 1,)),
        ],
        compiler_params=pltpu.CompilerParams(collective_id=0, has_side_effects=True),
    )(q, k, v, qg, kg, dk, dv, ids, counts, pages, pw, pg, ow)
    made = tuple(pltpu.with_memory_space_constraint(x, pltpu.VMEM) for x in made)
    return pl.pallas_call(
        write_out,
        out_shape=tuple(jax.ShapeDtypeStruct(x.shape, x.dtype) for x in made),
        in_specs=[pl.BlockSpec(memory_space=pltpu.VMEM)] * 2,
        out_specs=(pl.BlockSpec(memory_space=pltpu.HBM),) * 2,
        scratch_shapes=[pltpu.SemaphoreType.DMA((2,))],
    )(*made)


def solution(mesh):
    return jax.shard_map(
        fused_body if mesh.shape["block"] * 4 == 4 * GROUP else body,
        mesh=mesh,
        in_specs=(
            P(("groups", "shape"), "block", None),
            P(("groups", "shape"), "block", None),
            P(("groups", "shape"), "block", None),
            P(),
            P(),
            P(("groups", "shape"), "block", None),
            P(("groups", "shape"), "block", None),
            P(("groups", "shape"), "block"),
            P(("groups", "shape"), "block"),
            P(("groups", "shape"), "block"),
            P(),
            P(),
            P(),
        ),
        out_specs=(P(("groups", "shape"), "block", None), P(("groups", "shape"), "block", None)),
        check_vma=False,
    )
```

```python
import math

import jax
import jax.numpy as jnp
from jax import lax
from jax.experimental import pallas as pl
from jax.experimental.pallas import tpu as pltpu
from jax.sharding import PartitionSpec as P

FLOW_HEAD_COUNT = 16
FLOW_HEAD_SIZE = 128
DEC_HEADS = 16
DEC_HEAD = 64
NFREQ = 8
RES = 512
SIDE = 8
PAGES = 1
QB = 512
PER_SIDE = 64


def norm_per_head(values_in, gain, head_count):
    flat_rows = values_in.shape[0]
    entries = values_in.astype(jnp.float32).reshape(flat_rows, head_count, -1)
    scaled = entries * lax.rsqrt(jnp.mean(entries * entries, axis=-1, keepdims=True) + 1e-06)
    return (scaled * gain).reshape(flat_rows, -1).astype(jnp.bfloat16)


def query_points(block_id):
    point_index = jnp.arange(QB, dtype=jnp.int32)
    cell_index = [
        block_id // (PER_SIDE * PER_SIDE) * SIDE + point_index // (SIDE * SIDE),
        block_id // PER_SIDE % PER_SIDE * SIDE + point_index // SIDE % SIDE,
        block_id % PER_SIDE * SIDE + point_index % SIDE,
    ]
    coords = jnp.stack(
        [(cell.astype(jnp.float32) + 0.5) * (2.0 / RES) - 1.0 for cell in cell_index], 0
    )
    frequency = math.pi * 2.0 ** jnp.arange(NFREQ).astype(jnp.float32)
    phases = (coords[:, None, :] * frequency[None, :, None]).reshape(3 * NFREQ, QB)
    return jnp.concatenate([coords, jnp.sin(phases), jnp.cos(phases)], 0)


def decode_block(block_id, k_heads, v_heads, point_weight, point_gain, occupancy_weight):
    features = query_points(block_id)
    start_proj = lax.dot_general(
        features,
        point_weight,
        (((0,), (0,)), ((), ())),
        precision=lax.Precision.HIGHEST,
        preferred_element_type=jnp.float32,
    )
    row_mean = jnp.mean(start_proj, axis=-1, keepdims=True)
    centred = start_proj - row_mean
    row_var = jnp.mean(centred * centred, axis=-1, keepdims=True)
    point_query = (centred * lax.rsqrt(row_var + 1e-05) * point_gain).astype(jnp.bfloat16)
    q_heads = jnp.transpose(point_query.reshape(QB, DEC_HEADS, DEC_HEAD), (1, 0, 2))

    def one_head(head_item):
        q_head, k_head, v_head = head_item
        score_matrix = jnp.dot(q_head, k_head.T, preferred_element_type=jnp.float32) / math.sqrt(
            DEC_HEAD
        )
        row_maximum = jnp.max(score_matrix, axis=-1, keepdims=True)
        weights = jnp.exp(score_matrix - row_maximum)
        row_sum = jnp.sum(weights, axis=-1, keepdims=True)
        mixed = jnp.dot(weights.astype(jnp.bfloat16), v_head, preferred_element_type=jnp.float32)
        return mixed / row_sum

    per_head = lax.map(one_head, (q_heads, k_heads, v_heads))
    hidden = start_proj + jnp.transpose(per_head, (1, 0, 2)).reshape(QB, -1)
    hid_mean = jnp.mean(hidden, axis=-1, keepdims=True)
    hid_centred = hidden - hid_mean
    hid_var = jnp.mean(hid_centred * hid_centred, axis=-1, keepdims=True)
    normed = hid_centred * lax.rsqrt(hid_var + 1e-05)
    return jnp.dot(
        normed,
        occupancy_weight,
        precision=lax.Precision.HIGHEST,
        preferred_element_type=jnp.float32,
    )


def decode_many(id_list, owner_list, k_all, value_all, point_weight, point_gain, occupancy_weight):

    def one_block(block_item):
        block_id, owner_shape = block_item
        k_heads = lax.dynamic_index_in_dim(k_all, owner_shape, 0, keepdims=False)
        v_heads = lax.dynamic_index_in_dim(value_all, owner_shape, 0, keepdims=False)
        return decode_block(block_id, k_heads, v_heads, point_weight, point_gain, occupancy_weight)

    return lax.map(one_block, (id_list, owner_list))


def body(
    query,
    raw_flow_keys,
    flow_value_input,
    query_norm_gain,
    key_norm_gain,
    dec_keys,
    dec_values,
    block_ids,
    counts,
    page_of,
    point_weight,
    point_gain,
    occupancy_weight,
):
    shape_number, token_rows, feature_width = query.shape
    scale_per_head = 1.0 / math.sqrt(FLOW_HEAD_SIZE)
    normed_queries = norm_per_head(
        query.reshape(shape_number * token_rows, feature_width), query_norm_gain, FLOW_HEAD_COUNT
    )
    normed_queries = normed_queries.reshape(shape_number, token_rows, feature_width)
    normed_keys = norm_per_head(
        raw_flow_keys.reshape(shape_number * token_rows, feature_width),
        key_norm_gain,
        FLOW_HEAD_COUNT,
    )
    normed_keys = normed_keys.reshape(shape_number, token_rows, feature_width)
    latents = (
        lax.all_gather(dec_keys, "block", axis=1, tiled=True),
        lax.all_gather(dec_values, "block", axis=1, tiled=True),
    )
    peer_total = lax.axis_size("block")
    query_split = normed_queries.reshape(shape_number, token_rows, FLOW_HEAD_COUNT, FLOW_HEAD_SIZE)
    row_maximum = jnp.full((shape_number, FLOW_HEAD_COUNT, token_rows), -1e30, jnp.float32)
    k_piece = lax.all_gather(normed_keys, "block", axis=1, tiled=True).reshape(
        shape_number, -1, FLOW_HEAD_COUNT, FLOW_HEAD_SIZE
    )
    v_piece = lax.all_gather(flow_value_input, "block", axis=1, tiled=True).reshape(
        shape_number, -1, FLOW_HEAD_COUNT, FLOW_HEAD_SIZE
    )
    score_matrix = (
        jnp.einsum("sqhe,skhe->shqk", query_split, k_piece, preferred_element_type=jnp.float32)
        * scale_per_head
    )
    new_max = jnp.maximum(row_maximum, jnp.max(score_matrix, axis=-1))
    weights = jnp.exp(score_matrix - new_max[..., None])
    row_sum = jnp.sum(weights, axis=-1)
    mixed_sum = jnp.einsum(
        "shqk,skhe->shqe", weights.astype(jnp.bfloat16), v_piece, preferred_element_type=jnp.float32
    )
    row_maximum, row_sum, mixed_sum = (new_max, row_sum, mixed_sum)
    attended = mixed_sum / row_sum[..., None]
    flow_out = (
        jnp.transpose(attended, (0, 2, 1, 3))
        .reshape(shape_number, token_rows, feature_width)
        .astype(jnp.bfloat16)
    )
    key_rows, value_rows = latents
    k_all = jnp.transpose(key_rows.reshape(shape_number, -1, DEC_HEADS, DEC_HEAD), (0, 2, 1, 3))
    value_all = jnp.transpose(
        value_rows.reshape(shape_number, -1, DEC_HEADS, DEC_HEAD), (0, 2, 1, 3)
    )
    slot_count = block_ids.shape[1]
    slot_index = jnp.arange(slot_count, dtype=jnp.int32)
    live_mask = slot_index[None, :] < counts
    dest_peer = page_of // PAGES
    local_page = page_of % PAGES
    peer_ids = jnp.arange(peer_total, dtype=jnp.int32)
    route = (dest_peer[:, None, :] == peer_ids[None, :, None]) & live_mask[:, None, :]
    page_tag = jnp.where(
        jnp.any(route, axis=-1), jnp.sum(jnp.where(route, local_page[:, None, :], 0), axis=-1), -1
    )
    page_tag = jnp.transpose(page_tag)
    page_range = jnp.arange(PAGES, dtype=jnp.int32)
    send_ids = jnp.transpose(jnp.sum(jnp.where(route, block_ids[:, None, :], 0), axis=-1))
    recv_ids, recv_tag = (
        lax.all_to_all(send_ids, "block", split_axis=0, concat_axis=0, tiled=True),
        lax.all_to_all(page_tag, "block", split_axis=0, concat_axis=0, tiled=True),
    )
    page_match = recv_tag[None, :, :] == page_range[:, None, None]
    chosen = jnp.sum(jnp.where(page_match, recv_ids[None, :, :], 0), axis=1)
    present = jnp.transpose(jnp.any(page_match, axis=1))
    owner_list = jnp.repeat(jnp.arange(shape_number, dtype=jnp.int32), PAGES)
    occ_rows = decode_many(
        jnp.transpose(chosen).reshape(-1),
        owner_list,
        k_all,
        value_all,
        point_weight,
        point_gain,
        occupancy_weight,
    )
    occ_rows = occ_rows.reshape(shape_number, PAGES, QB)
    occupancy = jnp.where(present[:, :, None], occ_rows, jnp.zeros_like(occ_rows))
    return (flow_out, occupancy)


F32, BF16 = jnp.float32, jnp.bfloat16
MESH_ID = pl.DeviceIdType.MESH
WIDTH = DEC_HEADS * DEC_HEAD
FEATS = 3 + 6 * NFREQ
ROWS = 64
GROUP = 4
GROUPS = DEC_HEADS // GROUP
GW = GROUP * DEC_HEAD
CAP = 4


def split(x):
    hi = x.astype(BF16)
    return hi, (x - hi.astype(F32)).astype(BF16)


def dot(a, b, ca, cb, precision=None):
    return lax.dot_general(
        a, b, (((ca,), (cb,)), ((), ())), precision=precision, preferred_element_type=F32
    )


def sine(r):
    r = ((r + 512) & 1023) - 512
    r = jnp.where(r > 256, 512 - r, jnp.where(r < -256, -512 - r, r))
    x = r.astype(F32) * (math.pi / 512)
    x2 = x * x
    acc = jnp.full_like(x, 1.0 / math.factorial(13))
    for order in (11, 9, 7, 5, 3, 1):
        sign = 1.0 if order % 4 == 1 else -1.0
        acc = acc * x2 + sign / math.factorial(order)
    return acc * x


def fused_kernel(
    n, q_in, k_in, v_in, qg_in, kg_in, dk_in, dv_in, id_in, cnt_in, page_in, pw_in, pg_in, ow_in,
    flow_out, occ_out,
    q_b, kv_b, dkv_b, int_b, cnt_b, gain_b, vec_b, pw_b,
    w_s, wg_s, wx_s, gram_s, mid_s, near_s, far_s, qf_s, q_s, form_s, tok_s, rows_s, kf_s, vf_s,
    send_sem, recv_sem, local_sem, ready_sem,
):
    me = lax.axis_index("block")
    barrier = pltpu.get_barrier_semaphore()
    for peer in range(1, n):

        @pl.when(me < peer)
        def _():
            pl.semaphore_signal(barrier, inc=1, device_id={"block": peer}, device_id_type=MESH_ID)

    @pl.when(me > 0)
    def _():
        pl.semaphore_wait(barrier, me)

    early = [
        (id_in, int_b, 0, 0), (page_in, int_b, 1, 0), (cnt_in, cnt_b, None, 1),
        (dk_in.at[0], dkv_b, 0, 3), (dv_in.at[0], dkv_b, 1, 3),
    ]
    late = [(k_in.at[0], kv_b, 0, 2), (v_in.at[0], kv_b, 1, 2)]

    def mine(buf, part):
        return buf.at[me] if part is None else buf.at[me, part]

    def send(peer, moved):
        final = n - 1 if 2 * peer < n else 0
        for src, buf, part, kind in moved:
            into = kind
            out = 4 if peer == 0 and kind == 2 else kind
            if kind == 3:
                into = jnp.where(me == final, 5, jnp.where(me == peer - 1, 4, 3))
            pltpu.make_async_remote_copy(
                src_ref=src, dst_ref=mine(buf, part),
                send_sem=send_sem.at[out], recv_sem=recv_sem.at[into],
                device_id={"block": peer}, device_id_type=MESH_ID,
            ).start()

    for peer in range(n - 1):

        @pl.when(me > peer)
        def _():
            pl.semaphore_signal(
                ready_sem.at[me - 1], inc=1, device_id={"block": peer}, device_id_type=MESH_ID
            )
            send(peer, early)
            if peer == 0:
                send(peer, late)

    plain = [
        (pw_in, pw_b, 0), (pg_in, vec_b.at[0], 1), (ow_in, vec_b.at[1], 1),
        (q_in.at[0], q_b, 2), (qg_in, gain_b.at[0], 3), (kg_in, gain_b.at[1], 3),
    ]
    for src, dst, kind in plain:
        pltpu.make_async_copy(src, dst, local_sem.at[kind]).start()
    for src, buf, part, kind in early + late:
        pltpu.make_async_copy(src, mine(buf, part), recv_sem.at[kind]).start()

    def whole(ref, sem):
        pltpu.make_async_copy(ref, ref, sem).wait()

    whole(pw_b, local_sem.at[0])
    whole(vec_b, local_sem.at[1])
    whole(q_b, local_sem.at[2])
    whole(gain_b, local_sem.at[3])
    kinds = [int_b, cnt_b, kv_b, dkv_b]

    def arrive(kind):
        whole(kinds[kind], recv_sem.at[kind])

    w_s[...] = jnp.zeros_like(w_s)
    w_s[0:FEATS, :] = pw_b[...]
    w = w_s[...]
    centred = w - jnp.mean(w, axis=1, keepdims=True)
    ow = vec_b[1]
    twice = jnp.concatenate([centred, centred], 0)
    gram = dot(
        jnp.concatenate([centred, jnp.broadcast_to(ow * WIDTH, (16, WIDTH))], 0),
        twice, 1, 1, lax.Precision.HIGHEST,
    ) * (1.0 / WIDTH)
    g_hi, g_lo = split(gram)
    gram_s[...] = jnp.concatenate([g_hi, g_lo[:, 0:ROWS]], 1)
    for ref, values in ((wg_s, centred * (vec_b[0] * (1.0 / math.sqrt(DEC_HEAD)))), (wx_s, centred * 2.0)):
        ref[...] = values.astype(BF16)
    o_hi, o_lo = split(ow - jnp.mean(ow, axis=1, keepdims=True))
    line = lax.broadcasted_iota(jnp.int32, (16, WIDTH), 0)
    mid = jnp.where(line == 0, o_hi.astype(F32), jnp.where(line == 1, o_lo.astype(F32), 0.0))
    mid_s[...] = jnp.where(line == 2, 1.0 / WIDTH, mid).astype(BF16)

    rho = lax.broadcasted_iota(jnp.int32, (ROWS, QB), 0)
    lane = lax.broadcasted_iota(jnp.int32, (ROWS, QB), 1)
    which = jnp.where(rho < 3 + 3 * NFREQ, rho - 3, rho - 3 - 3 * NFREQ)
    dim = jnp.where(rho < 3, rho, which >> 3)
    mult = jnp.where(rho < 3, 1, jnp.left_shift(1, which & 7))
    offset = jnp.where(dim == 0, lane >> 6, jnp.where(dim == 1, (lane >> 3) & 7, lane & 7))
    base = (2 * offset + 1 - RES) * mult + jnp.where(rho >= 3 + 3 * NFREQ, RES // 2, 0)
    near_s[...] = jnp.where(rho < 3, base.astype(F32) * (1.0 / RES), jnp.where(rho < FEATS, sine(base), 0.0))
    far_s[...] = jnp.where(rho < 3, 1.0, jnp.where(rho < FEATS, sine(base + RES // 2), 0.0))

    per = q_b.shape[0]
    tokens = n * per
    pair = 2 * FLOW_HEAD_SIZE
    pick_r = lax.broadcasted_iota(jnp.int32, qf_s.shape, 0)
    pick_c = lax.broadcasted_iota(jnp.int32, qf_s.shape, 1)
    qf_s[...] = jnp.where((pick_r // per) % 4 == 2 + pick_c // FLOW_HEAD_SIZE, 1.0, 0.0)
    for h in range(FLOW_HEAD_COUNT):
        cols = slice(h * FLOW_HEAD_SIZE, (h + 1) * FLOW_HEAD_SIZE)
        x = q_b[:, cols].astype(F32)
        x = x * lax.rsqrt(jnp.mean(x * x, axis=-1, keepdims=True) + 1e-06) * (gain_b[0] * gain_b[1])
        row = (h // 2) * 4 * per + (h % 2) * per
        qf_s[row : row + per, (h % 2) * FLOW_HEAD_SIZE : (h % 2 + 1) * FLOW_HEAD_SIZE] = x
    q_s[...] = qf_s[...].astype(BF16)

    @pl.when(me > 0)
    def _():
        whole(kv_b.at[0], send_sem.at[4])

    for peer in range(1, n - 1):

        @pl.when(me > peer)
        def _():
            send(peer, late)

    for peer in range(1, n):

        @pl.when(me < peer)
        def _():
            pl.semaphore_wait(ready_sem.at[peer - 1], 1)
            send(peer, early)

    @pl.when(me == 0)
    def _():
        for peer in range(1, n):
            send(peer, late)
        whole(dkv_b.at[0 : n - 1], recv_sem.at[3])

    @pl.when(me > 0)
    def _():
        whole(dkv_b.at[0], recv_sem.at[4])

    for peer in range(2, n):

        @pl.when((me > 0) & (me < peer))
        def _():
            send(peer, late)

    @pl.when(me > 0)
    def _():
        whole(dkv_b.at[0 : n - 2], recv_sem.at[3])

    shift = jnp.where(2 * me < n, 0, 1)
    final = (n - 1) * (1 - shift)

    rows_g = GROUP * tokens
    span = 4 * per
    head_r = lax.broadcasted_iota(jnp.int32, (2, 2 * per, GW), 0) * 2
    head_r += lax.broadcasted_iota(jnp.int32, (2, 2 * per, GW), 1) & 1
    own_head = head_r == lax.broadcasted_iota(jnp.int32, (2, 2 * per, GW), 2) // DEC_HEAD
    tiles = WIDTH // 128

    def place(row, source):
        for part in range(2):
            x = dkv_b[source, part].astype(F32)
            for c in range(tiles):
                for twin in range(2):
                    tok_s[part * tiles + c, pl.ds(2 * per * row + twin, per, stride=2), :] = x[
                        :, c * 128 : (c + 1) * 128
                    ]
            for g in range(GROUPS):
                first = part * tiles + g * GW // 128
                y = jnp.concatenate(
                    [tok_s[first + i, 2 * per * row : 2 * per * (row + 1), :] for i in range(GW // 128)], 1
                )
                y = jnp.where(own_head, y[None], 0.0).reshape(span, GW).astype(BF16)
                rows_s[part * GROUPS + g, row * span : (row + 1) * span, :] = y

    for row in range(n - 1):
        place(row, row + shift)
    arrive(0)
    arrive(1)
    whole(dkv_b.at[0], recv_sem.at[5])
    place(n - 1, final)

    def left_of(b):
        b_hi, b_lo = split(b)
        return jnp.concatenate([b_hi, b_hi, b_lo], 1)

    left, right = [], []
    for g in range(GROUPS):
        cols = slice(g * GW, (g + 1) * GW)
        left.append(left_of(dot(rows_s[g], wg_s[:, cols], 1, 1)))
        vb = rows_s[GROUPS + g]
        right.append(left_of(dot(vb, wx_s[:, cols], 1, 1)))
        y = dot(jnp.concatenate([vb, mid_s[:, cols]], 0), vb, 1, 1)
        y_hi = y.astype(BF16).astype(F32)
        y_lo = y - y_hi
        form_s[g] = jnp.concatenate([y_hi[0:rows_g], y_lo[0:rows_g], y_hi[rows_g : rows_g + 8], y_lo[rows_g : rows_g + 8]], 0).astype(BF16)

    slot = lax.broadcasted_iota(jnp.int32, (1, CAP), 1)
    number = jnp.zeros((1, CAP), F32)
    for s in range(n):
        hit = (int_b[s, 1] == me) & (slot < cnt_b[s])
        number += jnp.where(hit, (int_b[s, 0] + 1).astype(F32), 0.0)
    number = jnp.sum(number, axis=1, keepdims=True)
    present = number > 0.5
    block = jnp.maximum(number - 1.0, 0.0).astype(jnp.int32)
    rows1 = lax.broadcasted_iota(jnp.int32, (ROWS, 128), 0)
    which1 = jnp.where(rows1 < 3 + 3 * NFREQ, rows1 - 3, rows1 - 3 - 3 * NFREQ)
    dim1 = jnp.where(rows1 < 3, rows1, which1 >> 3)
    mult1 = jnp.where(rows1 < 3, 1, jnp.left_shift(1, which1 & 7))
    cell = jnp.where(
        dim1 == 0, block >> 12, jnp.where(dim1 == 1, (block >> 6) & (PER_SIDE - 1), block & (PER_SIDE - 1))
    )
    cell = cell * mult1 * (2 * SIDE)
    turn = jnp.where(rows1 < 3, 1.0, sine(cell + RES // 2))
    step = jnp.where(rows1 < 3, cell.astype(F32) * (1.0 / RES), sine(cell))
    feats = near_s[...] * jnp.concatenate([turn] * (QB // 128), 1)
    feats += far_s[...] * jnp.concatenate([step] * (QB // 128), 1)
    f_hi, f_lo = split(feats)
    f3 = jnp.concatenate([f_hi, f_lo, f_hi], 0)

    scores = dot(jnp.concatenate(left + [gram_s[...]] + right, 0), f3, 1, 0)
    below = GROUPS * rows_g
    spread = jnp.sum(scores[below : below + ROWS] * feats, axis=0, keepdims=True)
    logit = scores[below + ROWS : below + ROWS + 1]
    rstd = lax.rsqrt(spread + 1e-05) * (1.0 / math.log(2.0))

    squares = jnp.zeros((8, QB), F32)
    linear = jnp.zeros((8, QB), F32)
    for g in range(GROUPS):
        score = scores[g * rows_g : (g + 1) * rows_g] * rstd
        score = score.reshape(n, 2, 2 * per, QB)
        top = jnp.max(score, axis=0)
        top = jnp.maximum(top, pltpu.roll(top, 4, 1))
        top = jnp.maximum(top, pltpu.roll(top, 2, 1))
        e = jnp.exp2(score - top[None])
        total = jnp.sum(e, axis=0)
        total = total + pltpu.roll(total, 4, 1)
        total = total + pltpu.roll(total, 2, 1)
        probs = (e * (1.0 / total)[None]).reshape(rows_g, QB).astype(BF16)
        out = dot(form_s[g], probs, 1, 0)
        cross = scores[below + ROWS + 16 + g * rows_g : below + ROWS + 16 + (g + 1) * rows_g]
        cross += out[0:rows_g] + out[rows_g : 2 * rows_g]
        squares += jnp.sum((cross * probs.astype(F32)).reshape(-1, 8, QB), axis=0)
        linear += out[2 * rows_g : 2 * rows_g + 8] + out[2 * rows_g + 8 :]
    mean = linear[2:3]
    logit += linear[0:1] + linear[1:2]
    var = spread + jnp.sum(squares, axis=0, keepdims=True) * (1.0 / WIDTH) - mean * mean
    occ = logit * lax.rsqrt(jnp.maximum(var, 0.0) + 1e-05)
    occ_out[0] = jnp.where(present, occ, 0.0)

    arrive(2)
    for s in range(n):
        kf_s[s * per : (s + 1) * per, :] = kv_b[s, 0].astype(F32)
        vf_s[s * per : (s + 1) * per, :] = kv_b[s, 1].astype(F32)
    score, size = [], []
    for r in range(FLOW_HEAD_COUNT // 2):
        keys = kf_s[:, r * pair : (r + 1) * pair]
        s_hi, s_lo = split(keys * keys)
        rows = q_s[r * 4 * per : (r + 1) * 4 * per, :]
        score.append(dot(rows, keys.astype(BF16), 1, 1)[0 : 2 * per])
        size.append((dot(rows, s_hi, 1, 1) + dot(rows, s_lo, 1, 1))[2 * per :])
    score, size = jnp.concatenate(score, 0), jnp.concatenate(size, 0)
    size = lax.rsqrt(size * (1.0 / FLOW_HEAD_SIZE) + 1e-06) * (1.0 / math.sqrt(FLOW_HEAD_SIZE))
    score = score * size
    weights = jnp.exp(score)
    inverse = 1.0 / jnp.sum(weights, axis=-1, keepdims=True)
    for r in range(FLOW_HEAD_COUNT // 2):
        cols = slice(2 * r * FLOW_HEAD_SIZE, 2 * (r + 1) * FLOW_HEAD_SIZE)
        rows = slice(2 * r * per, 2 * (r + 1) * per)
        mixed = dot(weights[rows].astype(BF16), vf_s[:, cols].astype(BF16), 1, 0) * inverse[rows]
        mixed = jnp.concatenate([mixed[0:per, 0:FLOW_HEAD_SIZE], mixed[per:, FLOW_HEAD_SIZE:]], 1)
        flow_out[0, :, cols] = mixed.astype(BF16)

    for kind, buf in enumerate(kinds):
        if kind != 2:
            whole(buf.at[0 : n - 1], send_sem.at[kind])

    @pl.when(me > 0)
    def _():
        whole(kv_b.at[0 : n - 2], send_sem.at[2])

    @pl.when(me == 0)
    def _():
        whole(kv_b.at[0 : n - 1], send_sem.at[2])


def write_out(flow_ref, occ_ref, flow_out, occ_out, sem):
    copies = [
        pltpu.make_async_copy(flow_ref, flow_out, sem.at[0]),
        pltpu.make_async_copy(occ_ref, occ_out, sem.at[1]),
    ]
    for copy in copies:
        copy.start()
    for copy in copies:
        copy.wait()


def fused_body(*args):
    (q, k, v, qg, kg, dk, dv, ids, counts, pages, pw, pg, ow) = args
    n = lax.axis_size("block")
    per = q.shape[1]
    tokens = n * per
    flow_width = q.shape[2]
    qg, kg, pg, ow = (x.reshape(1, -1) for x in (qg, kg, pg, ow))
    vmem = pltpu.VMEM
    made = pl.pallas_call(
        lambda *refs: fused_kernel(n, *refs),
        out_shape=(pltpu.VMEM(q.shape, BF16), pltpu.VMEM((1, PAGES, QB), F32)),
        in_specs=[pl.BlockSpec(memory_space=pltpu.HBM)] * 13,
        out_specs=(pl.BlockSpec(memory_space=pltpu.VMEM), pl.BlockSpec(memory_space=pltpu.VMEM)),
        scratch_shapes=[
            vmem((per, flow_width), BF16),
            vmem((n, 2, per, flow_width), BF16),
            vmem((n, 2, per, WIDTH), BF16),
            vmem((n, 2, 1, CAP), jnp.int32),
            vmem((n, 1, 1), jnp.int32),
            vmem((2, 1, FLOW_HEAD_SIZE), F32),
            vmem((2, 1, WIDTH), F32),
            vmem((FEATS, WIDTH), F32),
            vmem((ROWS, WIDTH), F32),
            vmem((ROWS, WIDTH), BF16),
            vmem((ROWS, WIDTH), BF16),
            vmem((ROWS + 16, 3 * ROWS), BF16),
            vmem((16, WIDTH), BF16),
            vmem((ROWS, QB), F32),
            vmem((ROWS, QB), F32),
            vmem((2 * FLOW_HEAD_COUNT * per, 2 * FLOW_HEAD_SIZE), F32),
            vmem((2 * FLOW_HEAD_COUNT * per, 2 * FLOW_HEAD_SIZE), BF16),
            vmem((GROUPS, 2 * GROUP * tokens + 16, ROWS), BF16),
            vmem((2 * WIDTH // 128, 2 * tokens, 128), F32),
            vmem((2 * GROUPS, GROUP * tokens, GW), BF16),
            vmem((tokens, flow_width), F32),
            vmem((tokens, flow_width), F32),
            pltpu.SemaphoreType.DMA((5,)),
            pltpu.SemaphoreType.DMA((6,)),
            pltpu.SemaphoreType.DMA((4,)),
            pltpu.SemaphoreType.REGULAR((n - 1,)),
        ],
        compiler_params=pltpu.CompilerParams(collective_id=0, has_side_effects=True),
    )(q, k, v, qg, kg, dk, dv, ids, counts, pages, pw, pg, ow)
    made = tuple(pltpu.with_memory_space_constraint(x, pltpu.VMEM) for x in made)
    return pl.pallas_call(
        write_out,
        out_shape=tuple(jax.ShapeDtypeStruct(x.shape, x.dtype) for x in made),
        in_specs=[pl.BlockSpec(memory_space=pltpu.VMEM)] * 2,
        out_specs=(pl.BlockSpec(memory_space=pltpu.HBM),) * 2,
        scratch_shapes=[pltpu.SemaphoreType.DMA((2,))],
    )(*made)


def solution(mesh):
    return jax.shard_map(
        fused_body if mesh.shape["block"] * 4 == 4 * GROUP else body,
        mesh=mesh,
        in_specs=(
            P(("groups", "shape"), "block", None),
            P(("groups", "shape"), "block", None),
            P(("groups", "shape"), "block", None),
            P(),
            P(),
            P(("groups", "shape"), "block", None),
            P(("groups", "shape"), "block", None),
            P(("groups", "shape"), "block"),
            P(("groups", "shape"), "block"),
            P(("groups", "shape"), "block"),
            P(),
            P(),
            P(),
        ),
        out_specs=(P(("groups", "shape"), "block", None), P(("groups", "shape"), "block", None)),
        check_vma=False,
    )
```

```python
import math

import jax
import jax.numpy as jnp
from jax import lax
from jax.experimental import pallas as pl
from jax.experimental.pallas import tpu as pltpu
from jax.sharding import PartitionSpec as P

FLOW_HEAD_COUNT = 16
FLOW_HEAD_SIZE = 128
DEC_HEADS = 16
DEC_HEAD = 64
NFREQ = 8
RES = 512
SIDE = 8
PAGES = 1
QB = 512
PER_SIDE = 64


def norm_per_head(values_in, gain, head_count):
    flat_rows = values_in.shape[0]
    entries = values_in.astype(jnp.float32).reshape(flat_rows, head_count, -1)
    scaled = entries * lax.rsqrt(jnp.mean(entries * entries, axis=-1, keepdims=True) + 1e-06)
    return (scaled * gain).reshape(flat_rows, -1).astype(jnp.bfloat16)


def query_points(block_id):
    point_index = jnp.arange(QB, dtype=jnp.int32)
    cell_index = [
        block_id // (PER_SIDE * PER_SIDE) * SIDE + point_index // (SIDE * SIDE),
        block_id // PER_SIDE % PER_SIDE * SIDE + point_index // SIDE % SIDE,
        block_id % PER_SIDE * SIDE + point_index % SIDE,
    ]
    coords = jnp.stack(
        [(cell.astype(jnp.float32) + 0.5) * (2.0 / RES) - 1.0 for cell in cell_index], 0
    )
    frequency = math.pi * 2.0 ** jnp.arange(NFREQ).astype(jnp.float32)
    phases = (coords[:, None, :] * frequency[None, :, None]).reshape(3 * NFREQ, QB)
    return jnp.concatenate([coords, jnp.sin(phases), jnp.cos(phases)], 0)


def decode_block(block_id, k_heads, v_heads, point_weight, point_gain, occupancy_weight):
    features = query_points(block_id)
    start_proj = lax.dot_general(
        features,
        point_weight,
        (((0,), (0,)), ((), ())),
        precision=lax.Precision.HIGHEST,
        preferred_element_type=jnp.float32,
    )
    row_mean = jnp.mean(start_proj, axis=-1, keepdims=True)
    centred = start_proj - row_mean
    row_var = jnp.mean(centred * centred, axis=-1, keepdims=True)
    point_query = (centred * lax.rsqrt(row_var + 1e-05) * point_gain).astype(jnp.bfloat16)
    q_heads = jnp.transpose(point_query.reshape(QB, DEC_HEADS, DEC_HEAD), (1, 0, 2))

    def one_head(head_item):
        q_head, k_head, v_head = head_item
        score_matrix = jnp.dot(q_head, k_head.T, preferred_element_type=jnp.float32) / math.sqrt(
            DEC_HEAD
        )
        row_maximum = jnp.max(score_matrix, axis=-1, keepdims=True)
        weights = jnp.exp(score_matrix - row_maximum)
        row_sum = jnp.sum(weights, axis=-1, keepdims=True)
        mixed = jnp.dot(weights.astype(jnp.bfloat16), v_head, preferred_element_type=jnp.float32)
        return mixed / row_sum

    per_head = lax.map(one_head, (q_heads, k_heads, v_heads))
    hidden = start_proj + jnp.transpose(per_head, (1, 0, 2)).reshape(QB, -1)
    hid_mean = jnp.mean(hidden, axis=-1, keepdims=True)
    hid_centred = hidden - hid_mean
    hid_var = jnp.mean(hid_centred * hid_centred, axis=-1, keepdims=True)
    normed = hid_centred * lax.rsqrt(hid_var + 1e-05)
    return jnp.dot(
        normed,
        occupancy_weight,
        precision=lax.Precision.HIGHEST,
        preferred_element_type=jnp.float32,
    )


def decode_many(id_list, owner_list, k_all, value_all, point_weight, point_gain, occupancy_weight):

    def one_block(block_item):
        block_id, owner_shape = block_item
        k_heads = lax.dynamic_index_in_dim(k_all, owner_shape, 0, keepdims=False)
        v_heads = lax.dynamic_index_in_dim(value_all, owner_shape, 0, keepdims=False)
        return decode_block(block_id, k_heads, v_heads, point_weight, point_gain, occupancy_weight)

    return lax.map(one_block, (id_list, owner_list))


def body(
    query,
    raw_flow_keys,
    flow_value_input,
    query_norm_gain,
    key_norm_gain,
    dec_keys,
    dec_values,
    block_ids,
    counts,
    page_of,
    point_weight,
    point_gain,
    occupancy_weight,
):
    shape_number, token_rows, feature_width = query.shape
    scale_per_head = 1.0 / math.sqrt(FLOW_HEAD_SIZE)
    normed_queries = norm_per_head(
        query.reshape(shape_number * token_rows, feature_width), query_norm_gain, FLOW_HEAD_COUNT
    )
    normed_queries = normed_queries.reshape(shape_number, token_rows, feature_width)
    normed_keys = norm_per_head(
        raw_flow_keys.reshape(shape_number * token_rows, feature_width),
        key_norm_gain,
        FLOW_HEAD_COUNT,
    )
    normed_keys = normed_keys.reshape(shape_number, token_rows, feature_width)
    latents = (
        lax.all_gather(dec_keys, "block", axis=1, tiled=True),
        lax.all_gather(dec_values, "block", axis=1, tiled=True),
    )
    peer_total = lax.axis_size("block")
    query_split = normed_queries.reshape(shape_number, token_rows, FLOW_HEAD_COUNT, FLOW_HEAD_SIZE)
    row_maximum = jnp.full((shape_number, FLOW_HEAD_COUNT, token_rows), -1e30, jnp.float32)
    k_piece = lax.all_gather(normed_keys, "block", axis=1, tiled=True).reshape(
        shape_number, -1, FLOW_HEAD_COUNT, FLOW_HEAD_SIZE
    )
    v_piece = lax.all_gather(flow_value_input, "block", axis=1, tiled=True).reshape(
        shape_number, -1, FLOW_HEAD_COUNT, FLOW_HEAD_SIZE
    )
    score_matrix = (
        jnp.einsum("sqhe,skhe->shqk", query_split, k_piece, preferred_element_type=jnp.float32)
        * scale_per_head
    )
    new_max = jnp.maximum(row_maximum, jnp.max(score_matrix, axis=-1))
    weights = jnp.exp(score_matrix - new_max[..., None])
    row_sum = jnp.sum(weights, axis=-1)
    mixed_sum = jnp.einsum(
        "shqk,skhe->shqe", weights.astype(jnp.bfloat16), v_piece, preferred_element_type=jnp.float32
    )
    row_maximum, row_sum, mixed_sum = (new_max, row_sum, mixed_sum)
    attended = mixed_sum / row_sum[..., None]
    flow_out = (
        jnp.transpose(attended, (0, 2, 1, 3))
        .reshape(shape_number, token_rows, feature_width)
        .astype(jnp.bfloat16)
    )
    key_rows, value_rows = latents
    k_all = jnp.transpose(key_rows.reshape(shape_number, -1, DEC_HEADS, DEC_HEAD), (0, 2, 1, 3))
    value_all = jnp.transpose(
        value_rows.reshape(shape_number, -1, DEC_HEADS, DEC_HEAD), (0, 2, 1, 3)
    )
    slot_count = block_ids.shape[1]
    slot_index = jnp.arange(slot_count, dtype=jnp.int32)
    live_mask = slot_index[None, :] < counts
    dest_peer = page_of // PAGES
    local_page = page_of % PAGES
    peer_ids = jnp.arange(peer_total, dtype=jnp.int32)
    route = (dest_peer[:, None, :] == peer_ids[None, :, None]) & live_mask[:, None, :]
    page_tag = jnp.where(
        jnp.any(route, axis=-1), jnp.sum(jnp.where(route, local_page[:, None, :], 0), axis=-1), -1
    )
    page_tag = jnp.transpose(page_tag)
    page_range = jnp.arange(PAGES, dtype=jnp.int32)
    send_ids = jnp.transpose(jnp.sum(jnp.where(route, block_ids[:, None, :], 0), axis=-1))
    recv_ids, recv_tag = (
        lax.all_to_all(send_ids, "block", split_axis=0, concat_axis=0, tiled=True),
        lax.all_to_all(page_tag, "block", split_axis=0, concat_axis=0, tiled=True),
    )
    page_match = recv_tag[None, :, :] == page_range[:, None, None]
    chosen = jnp.sum(jnp.where(page_match, recv_ids[None, :, :], 0), axis=1)
    present = jnp.transpose(jnp.any(page_match, axis=1))
    owner_list = jnp.repeat(jnp.arange(shape_number, dtype=jnp.int32), PAGES)
    occ_rows = decode_many(
        jnp.transpose(chosen).reshape(-1),
        owner_list,
        k_all,
        value_all,
        point_weight,
        point_gain,
        occupancy_weight,
    )
    occ_rows = occ_rows.reshape(shape_number, PAGES, QB)
    occupancy = jnp.where(present[:, :, None], occ_rows, jnp.zeros_like(occ_rows))
    return (flow_out, occupancy)


F32, BF16 = jnp.float32, jnp.bfloat16
MESH_ID = pl.DeviceIdType.MESH
WIDTH = DEC_HEADS * DEC_HEAD
FEATS = 3 + 6 * NFREQ
ROWS = 64
GROUP = 4
GROUPS = DEC_HEADS // GROUP
GW = GROUP * DEC_HEAD
CAP = 4


def split(x):
    hi = x.astype(BF16)
    return hi, (x - hi.astype(F32)).astype(BF16)


def dot(a, b, ca, cb, precision=None):
    return lax.dot_general(
        a, b, (((ca,), (cb,)), ((), ())), precision=precision, preferred_element_type=F32
    )


def sine(r):
    r = ((r + 512) & 1023) - 512
    r = jnp.where(r > 256, 512 - r, jnp.where(r < -256, -512 - r, r))
    x = r.astype(F32) * (math.pi / 512)
    x2 = x * x
    acc = jnp.full_like(x, 1.0 / math.factorial(13))
    for order in (11, 9, 7, 5, 3, 1):
        sign = 1.0 if order % 4 == 1 else -1.0
        acc = acc * x2 + sign / math.factorial(order)
    return acc * x


def fused_kernel(
    n, q_in, k_in, v_in, qg_in, kg_in, dk_in, dv_in, id_in, cnt_in, page_in, pw_in, pg_in, ow_in,
    flow_out, occ_out,
    q_b, kv_b, dkv_b, int_b, cnt_b, gain_b, vec_b, pw_b,
    w_s, wg_s, wx_s, gram_s, mid_s, near_s, far_s, qf_s, q_s, form_s, tok_s, rows_s, kf_s, vf_s,
    send_sem, recv_sem, local_sem, ready_sem,
):
    me = lax.axis_index("block")
    barrier = pltpu.get_barrier_semaphore()
    for peer in range(1, n):

        @pl.when(me < peer)
        def _():
            pl.semaphore_signal(barrier, inc=1, device_id={"block": peer}, device_id_type=MESH_ID)

    @pl.when(me > 0)
    def _():
        pl.semaphore_wait(barrier, me)

    early = [
        (id_in, int_b, 0, 0), (page_in, int_b, 1, 0), (cnt_in, cnt_b, None, 1),
        (dk_in.at[0], dkv_b, 0, 3), (dv_in.at[0], dkv_b, 1, 3),
    ]
    late = [(k_in.at[0], kv_b, 0, 2), (v_in.at[0], kv_b, 1, 2)]

    def mine(buf, part):
        return buf.at[me] if part is None else buf.at[me, part]

    def send(peer, moved):
        final = n - 1 if 2 * peer < n else 0
        for src, buf, part, kind in moved:
            into = kind
            out = 4 if peer == 0 and kind == 2 else kind
            if kind == 3:
                into = jnp.where(me == final, 5, jnp.where(me == peer - 1, 4, 3))
            pltpu.make_async_remote_copy(
                src_ref=src, dst_ref=mine(buf, part),
                send_sem=send_sem.at[out], recv_sem=recv_sem.at[into],
                device_id={"block": peer}, device_id_type=MESH_ID,
            ).start()

    for peer in range(n - 1):

        @pl.when(me > peer)
        def _():
            pl.semaphore_signal(
                ready_sem.at[me - 1], inc=1, device_id={"block": peer}, device_id_type=MESH_ID
            )
            send(peer, early)
            if peer == 0:
                send(peer, late)

    plain = [
        (pw_in, pw_b, 0), (pg_in, vec_b.at[0], 1), (ow_in, vec_b.at[1], 1),
        (q_in.at[0], q_b, 2), (qg_in, gain_b.at[0], 3), (kg_in, gain_b.at[1], 3),
    ]
    for src, dst, kind in plain:
        pltpu.make_async_copy(src, dst, local_sem.at[kind]).start()
    for src, buf, part, kind in early + late:
        pltpu.make_async_copy(src, mine(buf, part), recv_sem.at[kind]).start()

    def whole(ref, sem):
        pltpu.make_async_copy(ref, ref, sem).wait()

    whole(pw_b, local_sem.at[0])
    whole(vec_b, local_sem.at[1])
    whole(q_b, local_sem.at[2])
    whole(gain_b, local_sem.at[3])
    kinds = [int_b, cnt_b, kv_b, dkv_b]

    def arrive(kind):
        whole(kinds[kind], recv_sem.at[kind])

    w_s[...] = jnp.zeros_like(w_s)
    w_s[0:FEATS, :] = pw_b[...]
    w = w_s[...]
    centred = w - jnp.mean(w, axis=1, keepdims=True)
    ow = vec_b[1]
    twice = jnp.concatenate([centred, centred], 0)
    gram = dot(
        jnp.concatenate([centred, jnp.broadcast_to(ow * WIDTH, (16, WIDTH))], 0),
        twice, 1, 1, lax.Precision.HIGHEST,
    ) * (1.0 / WIDTH)
    g_hi, g_lo = split(gram)
    gram_s[...] = jnp.concatenate([g_hi, g_lo[:, 0:ROWS]], 1)
    for ref, values in ((wg_s, centred * (vec_b[0] * (1.0 / math.sqrt(DEC_HEAD)))), (wx_s, centred * 2.0)):
        ref[...] = values.astype(BF16)
    o_hi, o_lo = split(ow - jnp.mean(ow, axis=1, keepdims=True))
    line = lax.broadcasted_iota(jnp.int32, (16, WIDTH), 0)
    mid = jnp.where(line == 0, o_hi.astype(F32), jnp.where(line == 1, o_lo.astype(F32), 0.0))
    mid_s[...] = jnp.where(line == 2, 1.0 / WIDTH, mid).astype(BF16)

    rho = lax.broadcasted_iota(jnp.int32, (ROWS, QB), 0)
    lane = lax.broadcasted_iota(jnp.int32, (ROWS, QB), 1)
    which = jnp.where(rho < 3 + 3 * NFREQ, rho - 3, rho - 3 - 3 * NFREQ)
    dim = jnp.where(rho < 3, rho, which >> 3)
    mult = jnp.where(rho < 3, 1, jnp.left_shift(1, which & 7))
    offset = jnp.where(dim == 0, lane >> 6, jnp.where(dim == 1, (lane >> 3) & 7, lane & 7))
    base = (2 * offset + 1 - RES) * mult + jnp.where(rho >= 3 + 3 * NFREQ, RES // 2, 0)
    near_s[...] = jnp.where(rho < 3, base.astype(F32) * (1.0 / RES), jnp.where(rho < FEATS, sine(base), 0.0))
    far_s[...] = jnp.where(rho < 3, 1.0, jnp.where(rho < FEATS, sine(base + RES // 2), 0.0))

    per = q_b.shape[0]
    tokens = n * per
    pair = 2 * FLOW_HEAD_SIZE
    pick_r = lax.broadcasted_iota(jnp.int32, qf_s.shape, 0)
    pick_c = lax.broadcasted_iota(jnp.int32, qf_s.shape, 1)
    qf_s[...] = jnp.where((pick_r // per) % 4 == 2 + pick_c // FLOW_HEAD_SIZE, 1.0, 0.0)
    for h in range(FLOW_HEAD_COUNT):
        cols = slice(h * FLOW_HEAD_SIZE, (h + 1) * FLOW_HEAD_SIZE)
        x = q_b[:, cols].astype(F32)
        x = x * lax.rsqrt(jnp.mean(x * x, axis=-1, keepdims=True) + 1e-06) * (gain_b[0] * gain_b[1])
        row = (h // 2) * 4 * per + (h % 2) * per
        qf_s[row : row + per, (h % 2) * FLOW_HEAD_SIZE : (h % 2 + 1) * FLOW_HEAD_SIZE] = x
    q_s[...] = qf_s[...].astype(BF16)

    @pl.when(me > 0)
    def _():
        whole(kv_b.at[0], send_sem.at[4])

    for peer in range(1, n - 1):

        @pl.when(me > peer)
        def _():
            send(peer, late)

    for peer in range(1, n):

        @pl.when(me < peer)
        def _():
            pl.semaphore_wait(ready_sem.at[peer - 1], 1)
            send(peer, early)

    @pl.when(me == 0)
    def _():
        for peer in range(1, n):
            send(peer, late)
        whole(dkv_b.at[0 : n - 1], recv_sem.at[3])

    @pl.when(me > 0)
    def _():
        whole(dkv_b.at[0], recv_sem.at[4])

    for peer in range(2, n):

        @pl.when((me > 0) & (me < peer))
        def _():
            send(peer, late)

    @pl.when(me > 0)
    def _():
        whole(dkv_b.at[0 : n - 2], recv_sem.at[3])

    shift = jnp.where(2 * me < n, 0, 1)
    final = (n - 1) * (1 - shift)

    rows_g = GROUP * tokens
    span = 4 * per
    head_r = lax.broadcasted_iota(jnp.int32, (2, 2 * per, GW), 0) * 2
    head_r += lax.broadcasted_iota(jnp.int32, (2, 2 * per, GW), 1) & 1
    own_head = head_r == lax.broadcasted_iota(jnp.int32, (2, 2 * per, GW), 2) // DEC_HEAD
    tiles = WIDTH // 128

    def place(row, source):
        for part in range(2):
            x = dkv_b[source, part].astype(F32)
            for c in range(tiles):
                for twin in range(2):
                    tok_s[part * tiles + c, pl.ds(2 * per * row + twin, per, stride=2), :] = x[
                        :, c * 128 : (c + 1) * 128
                    ]
            for g in range(GROUPS):
                first = part * tiles + g * GW // 128
                y = jnp.concatenate(
                    [tok_s[first + i, 2 * per * row : 2 * per * (row + 1), :] for i in range(GW // 128)], 1
                )
                y = jnp.where(own_head, y[None], 0.0).reshape(span, GW).astype(BF16)
                rows_s[part * GROUPS + g, row * span : (row + 1) * span, :] = y

    for row in range(n - 1):
        place(row, row + shift)
    arrive(0)
    arrive(1)
    whole(dkv_b.at[0], recv_sem.at[5])
    place(n - 1, final)

    def left_of(b):
        b_hi, b_lo = split(b)
        return jnp.concatenate([b_hi, b_hi, b_lo], 1)

    left, right = [], []
    for g in range(GROUPS):
        cols = slice(g * GW, (g + 1) * GW)
        left.append(left_of(dot(rows_s[g], wg_s[:, cols], 1, 1)))
        vb = rows_s[GROUPS + g]
        right.append(left_of(dot(vb, wx_s[:, cols], 1, 1)))
        y = dot(jnp.concatenate([vb, mid_s[:, cols]], 0), vb, 1, 1)
        y_hi = y.astype(BF16).astype(F32)
        y_lo = y - y_hi
        form_s[g] = jnp.concatenate([y_hi[0:rows_g], y_lo[0:rows_g], y_hi[rows_g : rows_g + 8], y_lo[rows_g : rows_g + 8]], 0).astype(BF16)

    slot = lax.broadcasted_iota(jnp.int32, (1, CAP), 1)
    number = jnp.zeros((1, CAP), F32)
    for s in range(n):
        hit = (int_b[s, 1] == me) & (slot < cnt_b[s])
        number += jnp.where(hit, (int_b[s, 0] + 1).astype(F32), 0.0)
    number = jnp.sum(number, axis=1, keepdims=True)
    present = number > 0.5
    block = jnp.maximum(number - 1.0, 0.0).astype(jnp.int32)
    rows1 = lax.broadcasted_iota(jnp.int32, (ROWS, 128), 0)
    which1 = jnp.where(rows1 < 3 + 3 * NFREQ, rows1 - 3, rows1 - 3 - 3 * NFREQ)
    dim1 = jnp.where(rows1 < 3, rows1, which1 >> 3)
    mult1 = jnp.where(rows1 < 3, 1, jnp.left_shift(1, which1 & 7))
    cell = jnp.where(
        dim1 == 0, block >> 12, jnp.where(dim1 == 1, (block >> 6) & (PER_SIDE - 1), block & (PER_SIDE - 1))
    )
    cell = cell * mult1 * (2 * SIDE)
    turn = jnp.where(rows1 < 3, 1.0, sine(cell + RES // 2))
    step = jnp.where(rows1 < 3, cell.astype(F32) * (1.0 / RES), sine(cell))
    feats = near_s[...] * jnp.concatenate([turn] * (QB // 128), 1)
    feats += far_s[...] * jnp.concatenate([step] * (QB // 128), 1)
    f_hi, f_lo = split(feats)
    f3 = jnp.concatenate([f_hi, f_lo, f_hi], 0)

    scores = dot(jnp.concatenate(left + [gram_s[...]] + right, 0), f3, 1, 0)
    below = GROUPS * rows_g
    spread = jnp.sum(scores[below : below + ROWS] * feats, axis=0, keepdims=True)
    logit = scores[below + ROWS : below + ROWS + 1]
    rstd = lax.rsqrt(spread + 1e-05) * (1.0 / math.log(2.0))

    squares = jnp.zeros((8, QB), F32)
    linear = jnp.zeros((8, QB), F32)
    for g in range(GROUPS):
        score = scores[g * rows_g : (g + 1) * rows_g]
        score = score.reshape(n, 2, 2 * per, QB)
        top = jnp.max(score, axis=0)
        top = jnp.maximum(top, pltpu.roll(top, 4, 1))
        top = jnp.maximum(top, pltpu.roll(top, 2, 1))
        e = jnp.exp2((score - top[None]) * rstd)
        total = jnp.sum(e, axis=0)
        total = total + pltpu.roll(total, 4, 1)
        total = total + pltpu.roll(total, 2, 1)
        probs = (e * (1.0 / total)[None]).reshape(rows_g, QB).astype(BF16)
        out = dot(form_s[g], probs, 1, 0)
        cross = scores[below + ROWS + 16 + g * rows_g : below + ROWS + 16 + (g + 1) * rows_g]
        cross += out[0:rows_g] + out[rows_g : 2 * rows_g]
        squares += jnp.sum((cross * probs.astype(F32)).reshape(-1, 8, QB), axis=0)
        linear += out[2 * rows_g : 2 * rows_g + 8] + out[2 * rows_g + 8 :]
    mean = linear[2:3]
    logit += linear[0:1] + linear[1:2]
    var = spread + jnp.sum(squares, axis=0, keepdims=True) * (1.0 / WIDTH) - mean * mean
    occ = logit * lax.rsqrt(jnp.maximum(var, 0.0) + 1e-05)
    occ_out[0] = jnp.where(present, occ, 0.0)

    arrive(2)
    for s in range(n):
        kf_s[s * per : (s + 1) * per, :] = kv_b[s, 0].astype(F32)
        vf_s[s * per : (s + 1) * per, :] = kv_b[s, 1].astype(F32)
    score, size = [], []
    for r in range(FLOW_HEAD_COUNT // 2):
        keys = kf_s[:, r * pair : (r + 1) * pair]
        s_hi, s_lo = split(keys * keys)
        rows = q_s[r * 4 * per : (r + 1) * 4 * per, :]
        score.append(dot(rows, keys.astype(BF16), 1, 1)[0 : 2 * per])
        size.append((dot(rows, s_hi, 1, 1) + dot(rows, s_lo, 1, 1))[2 * per :])
    score, size = jnp.concatenate(score, 0), jnp.concatenate(size, 0)
    size = lax.rsqrt(size * (1.0 / FLOW_HEAD_SIZE) + 1e-06) * (1.0 / math.sqrt(FLOW_HEAD_SIZE))
    score = score * size
    weights = jnp.exp(score)
    inverse = 1.0 / jnp.sum(weights, axis=-1, keepdims=True)
    for r in range(FLOW_HEAD_COUNT // 2):
        cols = slice(2 * r * FLOW_HEAD_SIZE, 2 * (r + 1) * FLOW_HEAD_SIZE)
        rows = slice(2 * r * per, 2 * (r + 1) * per)
        mixed = dot(weights[rows].astype(BF16), vf_s[:, cols].astype(BF16), 1, 0) * inverse[rows]
        mixed = jnp.concatenate([mixed[0:per, 0:FLOW_HEAD_SIZE], mixed[per:, FLOW_HEAD_SIZE:]], 1)
        flow_out[0, :, cols] = mixed.astype(BF16)

    for kind, buf in enumerate(kinds):
        if kind != 2:
            whole(buf.at[0 : n - 1], send_sem.at[kind])

    @pl.when(me > 0)
    def _():
        whole(kv_b.at[0 : n - 2], send_sem.at[2])

    @pl.when(me == 0)
    def _():
        whole(kv_b.at[0 : n - 1], send_sem.at[2])


def write_out(flow_ref, occ_ref, flow_out, occ_out, sem):
    copies = [
        pltpu.make_async_copy(flow_ref, flow_out, sem.at[0]),
        pltpu.make_async_copy(occ_ref, occ_out, sem.at[1]),
    ]
    for copy in copies:
        copy.start()
    for copy in copies:
        copy.wait()


def fused_body(*args):
    (q, k, v, qg, kg, dk, dv, ids, counts, pages, pw, pg, ow) = args
    n = lax.axis_size("block")
    per = q.shape[1]
    tokens = n * per
    flow_width = q.shape[2]
    qg, kg, pg, ow = (x.reshape(1, -1) for x in (qg, kg, pg, ow))
    vmem = pltpu.VMEM
    made = pl.pallas_call(
        lambda *refs: fused_kernel(n, *refs),
        out_shape=(pltpu.VMEM(q.shape, BF16), pltpu.VMEM((1, PAGES, QB), F32)),
        in_specs=[pl.BlockSpec(memory_space=pltpu.HBM)] * 13,
        out_specs=(pl.BlockSpec(memory_space=pltpu.VMEM), pl.BlockSpec(memory_space=pltpu.VMEM)),
        scratch_shapes=[
            vmem((per, flow_width), BF16),
            vmem((n, 2, per, flow_width), BF16),
            vmem((n, 2, per, WIDTH), BF16),
            vmem((n, 2, 1, CAP), jnp.int32),
            vmem((n, 1, 1), jnp.int32),
            vmem((2, 1, FLOW_HEAD_SIZE), F32),
            vmem((2, 1, WIDTH), F32),
            vmem((FEATS, WIDTH), F32),
            vmem((ROWS, WIDTH), F32),
            vmem((ROWS, WIDTH), BF16),
            vmem((ROWS, WIDTH), BF16),
            vmem((ROWS + 16, 3 * ROWS), BF16),
            vmem((16, WIDTH), BF16),
            vmem((ROWS, QB), F32),
            vmem((ROWS, QB), F32),
            vmem((2 * FLOW_HEAD_COUNT * per, 2 * FLOW_HEAD_SIZE), F32),
            vmem((2 * FLOW_HEAD_COUNT * per, 2 * FLOW_HEAD_SIZE), BF16),
            vmem((GROUPS, 2 * GROUP * tokens + 16, ROWS), BF16),
            vmem((2 * WIDTH // 128, 2 * tokens, 128), F32),
            vmem((2 * GROUPS, GROUP * tokens, GW), BF16),
            vmem((tokens, flow_width), F32),
            vmem((tokens, flow_width), F32),
            pltpu.SemaphoreType.DMA((5,)),
            pltpu.SemaphoreType.DMA((6,)),
            pltpu.SemaphoreType.DMA((4,)),
            pltpu.SemaphoreType.REGULAR((n - 1,)),
        ],
        compiler_params=pltpu.CompilerParams(collective_id=0, has_side_effects=True),
    )(q, k, v, qg, kg, dk, dv, ids, counts, pages, pw, pg, ow)
    made = tuple(pltpu.with_memory_space_constraint(x, pltpu.VMEM) for x in made)
    return pl.pallas_call(
        write_out,
        out_shape=tuple(jax.ShapeDtypeStruct(x.shape, x.dtype) for x in made),
        in_specs=[pl.BlockSpec(memory_space=pltpu.VMEM)] * 2,
        out_specs=(pl.BlockSpec(memory_space=pltpu.HBM),) * 2,
        scratch_shapes=[pltpu.SemaphoreType.DMA((2,))],
    )(*made)


def solution(mesh):
    return jax.shard_map(
        fused_body if mesh.shape["block"] * 4 == 4 * GROUP else body,
        mesh=mesh,
        in_specs=(
            P(("groups", "shape"), "block", None),
            P(("groups", "shape"), "block", None),
            P(("groups", "shape"), "block", None),
            P(),
            P(),
            P(("groups", "shape"), "block", None),
            P(("groups", "shape"), "block", None),
            P(("groups", "shape"), "block"),
            P(("groups", "shape"), "block"),
            P(("groups", "shape"), "block"),
            P(),
            P(),
            P(),
        ),
        out_specs=(P(("groups", "shape"), "block", None), P(("groups", "shape"), "block", None)),
        check_vma=False,
    )
```
